768 devices in a mesh: wide: 48 (over y_hi, z, core), tensor: 16 (over y_lo, x).
Axes of the slice: x: 4, y: 8 (y_hi: 2, y_lo: 4; y = y_hi * 4 + y_lo), z: 12, core: 2. Of those that a mesh axis runs over, the one named last changes fastest.
Arguments:
- hidden: bfloat16 [73728, 3072], P('wide', 'tensor'), may hold values from -6 to 6
- modulation: float32 [2, 3072], P(None, 'tensor'), may hold values from -3 to 3
- final_weight: bfloat16 [3072, 64], P('tensor'), may hold values from -0.109375 to 0.109375
- noisy: float32 [73728, 64], P('wide'), may hold values from -6 to 6
- step_index: int32 [1], replicated, may hold values from 1 to 28
- slab_table: int32 [1152], P('wide'), may hold values from 0 to 47, as said below
- conv_in_weight: bfloat16 [144, 512], P(None, 'tensor'), may hold values from -0.5 to 0.5
- conv_in_bias: float32 [512], P('tensor'), may hold values from -3 to 3
- conv1_weight: bfloat16 [9, 512, 512], replicated, may hold values from -0.09375 to 0.09375
- conv1_bias: float32 [512], replicated, may hold values from -3 to 3
Outputs:
- decoder_features: bfloat16 [2304, 512, 128], P('wide', 'tensor')
- residual_branch: bfloat16 [2304, 512, 128], P('wide', 'tensor')
The draws below stay inside these ranges and needn't reach their ends.
Inputs may be any that keep to these rules, and one draw needn't show every extreme that they name: There are 24 distinct offsets o_j, one per local row j, with slab_table[w * 24 + j] = (w - o_j) modulo the number of wide devices: each slab receives each local row index from exactly one wide device, and the rows of one device go to distinct slabs. One of the offsets is half the number of wide devices (rounded down).
All inputs are finite; a program needn't handle non-finite values.
Results may differ from the reference program's by a relative error of at most 0.012.
Values may be sent and summed in bfloat16 or wider, within the bound.
No kernel may reach another device: no remote copies, remote signals or barrier semaphores. Data moves between devices by JAX's collectives and lax.ppermute only.
A program may use at most 64 MiB of HBM per device.

```python
import jax
import jax.numpy as jnp
from jax import lax

D = 3072
LC = 16
COUT = 512
GRID = 64
STEPS = 28
ROWS_DEV = 24
P_SIZE = 64
WPIX = 128
TOKEN_ROWS = 1152
TOKENS = 73728
PIXROWS = 2304
IMAGES = 18


def draw_slab_table(key, part):
    slabs = TOKEN_ROWS // ROWS_DEV
    half = slabs // 2
    steps_away = jax.random.permutation(jax.random.fold_in(key, 1), slabs - 1)[:ROWS_DEV - 1].astype(jnp.int32) + 1
    chosen = jnp.concatenate([jnp.zeros((1,), jnp.int32), steps_away])
    offsets = (half + chosen) % slabs
    order = jax.random.permutation(jax.random.fold_in(key, 2), ROWS_DEV).astype(jnp.int32)
    offsets = offsets[order].astype(jnp.int32)
    owners = jnp.arange(slabs, dtype=jnp.int32)[:, None]
    return ((owners - offsets[None, :]) % slabs).reshape(-1).astype(jnp.int32)


def block_levels(rng, extent, shards, least, top_value):
    factor_of = 1.0
    for axis_at, parts in shards:
        steps = jax.random.uniform(jax.random.fold_in(jax.random.fold_in(rng, 6), axis_at), (parts,), jnp.float32, least / len(shards), top_value / len(shards))
        factor_of = factor_of * jnp.repeat(jnp.exp(steps), extent[axis_at] // parts).reshape((-1,) + (1,) * (len(extent) - 1 - axis_at))
    return factor_of


def bell_draw(key, shape, scale, most, pieces=(), kind=jnp.bfloat16):
    loudness = block_levels(key, shape, pieces, -0.22, 0.18) if pieces else 1.0
    drawn = jax.random.normal(key, shape, jnp.float32) * scale * loudness
    return jnp.minimum(jnp.maximum(drawn, -most), most).astype(kind)


def setup_inputs(seed: int = 0) -> dict:
    seeds = jax.random.split(jax.random.key(seed), 11)
    hidden = bell_draw(seeds[0], (TOKENS, D), 1.0, 6.0, ((0, 48), (1, 16)))
    modulation = bell_draw(seeds[1], (2, D), 0.5, 3.0, ((1, 16),), jnp.float32)
    final_weight = bell_draw(seeds[2], (D, P_SIZE), D ** -0.5, 0.109375, ((0, 16),))
    noisy = bell_draw(seeds[3], (TOKENS, P_SIZE), 1.0, 6.0, ((0, 48),), jnp.float32)
    step_index = jax.random.randint(seeds[4], (1,), 1, STEPS + 1).astype(jnp.int32)
    slab_table = draw_slab_table(jax.random.fold_in(seeds[10], 71), 0)
    conv_in_weight = bell_draw(seeds[6], (9 * LC, COUT), (9 * LC) ** -0.5, 0.5, ((1, 16),))
    conv_in_bias = bell_draw(seeds[7], (COUT,), 0.5, 3.0, ((0, 16),), jnp.float32)
    conv1_weight = bell_draw(seeds[8], (9, COUT, COUT), (9 * COUT) ** -0.5, 0.09375)
    conv1_bias = bell_draw(seeds[9], (COUT,), 0.5, 3.0, (), jnp.float32)
    return {"hidden": hidden, "modulation": modulation, "final_weight": final_weight, "noisy": noisy, "step_index": step_index, "slab_table": slab_table, "conv_in_weight": conv_in_weight, "conv_in_bias": conv_in_bias, "conv1_weight": conv1_weight, "conv1_bias": conv1_bias}


shift_value = 3.0
norm_eps = 1e-06

def image_conv(images, kernel):
    return lax.conv_general_dilated(images, kernel, (1, 1), 'SAME', dimension_numbers=('NHWC', 'HWIO', 'NHWC'), precision=lax.Precision.HIGHEST)

def reference(hidden, modulation, final_weight, noisy, step_index, slab_table, conv_in_weight, conv_in_bias, conv1_weight, conv1_bias):
    feats = hidden.astype(jnp.float32)
    mean = lax.optimization_barrier(jnp.mean(feats, axis=-1, keepdims=True))
    var = lax.optimization_barrier(jnp.mean(feats * feats, axis=-1, keepdims=True)) - mean * mean
    rstd = 1.0 / jnp.sqrt(var + norm_eps)
    normed = (feats - mean) * rstd * (1.0 + modulation[1]) + modulation[0]
    velocity = jnp.dot(normed, final_weight.astype(jnp.float32), precision=lax.Precision.HIGHEST)
    frac = step_index[0].astype(jnp.float32) / STEPS
    sigma = shift_value * frac / (1.0 + (shift_value - 1.0) * frac)
    clean = (noisy - sigma * velocity).astype(jnp.bfloat16)
    rows = clean.reshape(TOKEN_ROWS, GRID * P_SIZE)
    local_row = (jnp.arange(TOKEN_ROWS) % ROWS_DEV).astype(jnp.int32)
    target = slab_table.astype(jnp.int32) * ROWS_DEV + local_row
    ordered = jnp.zeros_like(rows).at[target].set(rows)
    latent_image = ordered.reshape(TOKEN_ROWS, GRID, 2, 2, LC).transpose(0, 2, 1, 3, 4).reshape(IMAGES, WPIX, WPIX, LC)
    kernel_in = conv_in_weight.astype(jnp.float32).reshape(3, 3, LC, COUT)
    first = image_conv(latent_image.astype(jnp.float32), kernel_in) + conv_in_bias
    features = first.astype(jnp.bfloat16)
    activated = jax.nn.silu(features.astype(jnp.float32)).astype(jnp.bfloat16)
    kernel_one = conv1_weight.astype(jnp.float32).reshape(3, 3, COUT, COUT)

    def one_image(image):
        return (image_conv(image[None].astype(jnp.float32), kernel_one)[0] + conv1_bias).astype(jnp.bfloat16)
    second = lax.map(one_image, activated)
    decoder_features = features.transpose(0, 1, 3, 2).reshape(PIXROWS, COUT, WPIX)
    residual_branch = second.transpose(0, 1, 3, 2).reshape(PIXROWS, COUT, WPIX)
    return (decoder_features, residual_branch)
```

```python
import functools

import jax
import jax.numpy as jnp
from jax import lax
from jax.experimental import pallas as pl
from jax.experimental.pallas import tpu as pltpu
from jax.sharding import PartitionSpec as P

D = 3072
LC = 16
GRID = 64
STEPS = 28
WPIX = 128
shift_value = 3.0
norm_eps = 1e-06

F32 = jnp.float32
BF16 = jnp.bfloat16

SR = 24
STAT = 2 * SR
WROW = STAT + 32
BLOCK = WROW + 32


def iota(shape, dim):
    return lax.broadcasted_iota(jnp.int32, shape, dim)


def thirds(value):
    first = value.astype(BF16).astype(F32)
    rest = value - first
    second = rest.astype(BF16).astype(F32)
    return (first, second, (rest - second).astype(BF16).astype(F32))


def to_column(row):
    n = row.shape[1]
    return jnp.sum(jnp.where(iota((n, n), 0) == iota((n, n), 1), row, 0.0), axis=1, keepdims=True)


def to_row(column):
    n = column.shape[0]
    return jnp.sum(jnp.where(iota((n, n), 0) == iota((n, n), 1), column, 0.0), axis=0, keepdims=True)


def project_kernel(rows, peers, here, h_ref, mod_ref, w_ref, win_ref, bin_ref, noisy_ref, send_ref, noisy_out, sums, drawn):
    per = GRID // peers
    feats = h_ref.shape[0]
    weight = w_ref[...].astype(F32)
    scaled = (1.0 + mod_ref[1:2, :]) * weight
    colsum = jnp.sum(scaled, axis=1, keepdims=True)
    shifted = jnp.sum(mod_ref[0:1, :] * weight, axis=1, keepdims=True)
    left = jnp.concatenate(thirds(scaled - colsum / feats), axis=0).astype(BF16)
    lane = iota((1, 128), 1)
    low = lane < 64
    step = 256
    for at in range(0, h_ref.shape[1], step):
        hid = h_ref[:, at : at + step]
        prod = jnp.dot(left, hid, preferred_element_type=F32)
        wide = hid.astype(F32)
        pieces = thirds(jnp.sum(wide, axis=0, keepdims=True)) + thirds(jnp.sum(wide * wide, axis=0, keepdims=True))
        stats = [jnp.broadcast_to(p, (4, step)) for p in pieces] + [jnp.zeros((40, step), F32)]
        both = jnp.concatenate([prod[:64, :] + prod[64:128, :] + prod[128:, :]] + stats, axis=0)
        sums[at : at + step, :] = jnp.transpose(both)
        drawn[at : at + step, :] = jnp.transpose(noisy_ref[:, at : at + step])
    win = win_ref[...].astype(F32)
    outs = win.shape[0]
    rest_w = jnp.concatenate([win[:, 128:], jnp.zeros((outs, 128 - (win.shape[1] - 128)), F32)], axis=1)
    side = pltpu.roll(rest_w, 64, 1)
    for n, piece in enumerate(thirds(to_column(bin_ref[...]))):
        side = jnp.where(lane == 80 + n, piece, side)
    pad = jnp.zeros((1, 64), F32)
    lines = thirds(to_row(colsum)) + thirds(to_row(shifted))
    extra = jnp.concatenate([jnp.concatenate([v, pad], axis=1) for v in lines] + [jnp.zeros((2, 128), F32)], axis=0)
    main_w = win_ref[:, :128]
    fill = [jnp.zeros((SR - rows, 128), F32)] if rows < SR else []
    for peer in range(peers):
        base = peer * BLOCK
        stat = jnp.zeros((SR, 128), F32)
        halves = []
        for dk in range(per):
            val = sums[pl.ds(peer * per + dk, rows, stride=GRID), :]
            val = jnp.concatenate([val] + fill, axis=0) if fill else val
            turned = pltpu.roll(val, 64, 1)
            stat = jnp.where((lane % 4 == dk) & (lane < 24), turned, stat)
            halves.append(val if dk % 2 == 0 else turned)
        for half in range(per // 2):
            joined = jnp.where(low, halves[2 * half], halves[2 * half + 1])
            send_ref[base + half * SR : base + (half + 1) * SR, :] = joined.astype(BF16)
        tile = jnp.concatenate([stat, extra], axis=0) + side
        send_ref[base + STAT : base + STAT + 32, :] = tile.astype(BF16)
        send_ref[base + WROW : base + WROW + 32, :] = main_w
    mine = here[0] * per
    for half in range(per // 2):
        one = drawn[pl.ds(mine + 2 * half, rows, stride=GRID), :]
        two = drawn[pl.ds(mine + 2 * half + 1, rows, stride=GRID), :]
        both = jnp.concatenate([one, two], axis=1)
        noisy_out[half * SR : (half + 1) * SR, :] = jnp.concatenate([both] + fill, axis=0) if fill else both


def spread(tile, at, low):
    parts = []
    for half in range(2):
        a = tile[:, at + 2 * half : at + 2 * half + 1]
        b = tile[:, at + 2 * half + 1 : at + 2 * half + 2]
        parts.append(jnp.where(low, a, b))
    return jnp.concatenate(parts, axis=0)


def clean_kernel(rows, peers, slabs, feats, step_ref, table, recv_ref, noisy_ref, send_ref):
    lane = iota((1, 128), 1)
    low = lane < 64
    total = jnp.zeros((2 * SR, 128), F32)
    means = []
    columns = []
    sums = jnp.zeros((SR, 128), F32)
    shifted = jnp.zeros((1, 128), F32)
    for peer in range(peers):
        base = peer * BLOCK
        total = total + recv_ref[base : base + 2 * SR, :].astype(F32)
        tile = recv_ref[base + STAT : base + STAT + 32, :].astype(F32)
        stat = tile[:SR, :]
        stat = stat + pltpu.roll(stat, 124, 1) + pltpu.roll(stat, 120, 1)
        sums = sums + stat
        means.append(stat / feats)
        cs = jnp.where(low, tile[SR : SR + 1, :] + tile[SR + 1 : SR + 2, :] + tile[SR + 2 : SR + 3, :], 0.0)
        columns.append(cs + pltpu.roll(cs, 64, 1))
        sw = jnp.where(low, tile[SR + 3 : SR + 4, :] + tile[SR + 4 : SR + 5, :] + tile[SR + 5 : SR + 6, :], 0.0)
        shifted = shifted + sw + pltpu.roll(sw, 64, 1)
    mean = sums / (feats * peers)
    for m, cs in zip(means, columns):
        total = total + spread(m - mean, 0, low) * cs
    square = pltpu.roll(mean, 116, 1)
    rstd = 1.0 / jnp.sqrt(square - mean * mean + norm_eps)
    velocity = total * spread(rstd, 0, low) + shifted
    frac = jnp.zeros((1, 128), F32) + step_ref[0].astype(F32)
    frac = frac / STEPS
    sigma = shift_value * frac / (1.0 + (shift_value - 1.0) * frac)
    clean = (noisy_ref[...] - sigma * velocity).astype(BF16).astype(F32)
    held = jnp.concatenate([clean, pltpu.roll(clean, 64, 1), jnp.zeros((128 - 4 * SR, 128), F32)], axis=0).astype(BF16)
    owner = jnp.full((1, 128), -9, jnp.int32)
    for j in range(rows):
        owner = jnp.where((lane % SR == j) & (lane < 4 * SR), table[j], owner)
    shape = (slabs * 8, 128)
    row = iota(shape, 0)
    col = iota(shape, 1)
    slab = row // 8
    upper = row % 8 < 4
    dk = row % 4
    turned = col // (2 * SR)
    half = (col // SR) % 2
    j = col % SR
    right_half = half == dk // 2
    target = jnp.where(upper, owner, jnp.where(j == 0, owner - 1, -9))
    own = target == slab
    take_low = (right_half & (turned == dk % 2) & own).astype(F32).astype(BF16)
    above = upper & (j == rows - 1) & (owner + 1 == slab) & (owner >= 0)
    take_high = (right_half & (turned == 1 - dk % 2) & above).astype(F32).astype(BF16)
    left = jnp.dot(take_low, held, preferred_element_type=F32)
    right = jnp.dot(take_high, held, preferred_element_type=F32)
    send_ref[...] = jnp.where(low, left, right).astype(BF16)


def pick_kernel(rows, peers, slabs, here, table, recv_ref, send_ref, wide):
    wide[...] = recv_ref[...].astype(F32)
    lane = iota((8, 128), 1)
    low = lane < 64
    top = iota((8, 128), 0) < 4
    count = rows + 2
    per = count // 2

    def source(j):
        return lax.rem(2 * here[1] - table[j] + 2 * slabs, slabs)

    def piece(i, at_low, at_top):
        if i == 0:
            x, is_low, is_top = (lax.rem(source(rows - 1) - 1 + slabs, slabs), False, True)
        elif i == count - 1:
            x, is_low, is_top = (lax.rem(source(0) + 1, slabs), True, False)
        else:
            x, is_low, is_top = (source(i - 1), True, True)
        tile = wide[pl.ds(pl.multiple_of(x * 8, 8), 8), :]
        if is_low != at_low:
            tile = pltpu.roll(tile, 64, 1)
        if is_top != at_top:
            tile = pltpu.roll(tile, 4, 0)
        return tile

    for block in range((per + 1) // 2):
        quarters = []
        for at_top in (True, False):
            for at_low in (True, False):
                n = 2 * block + (0 if at_low else 1)
                if n < per:
                    quarters.append(piece(n + (0 if at_top else per), at_low, at_top))
                else:
                    quarters.append(jnp.zeros((8, 128), F32))
        tile = jnp.where(top, jnp.where(low, quarters[0], quarters[1]), jnp.where(low, quarters[2], quarters[3]))
        tile = tile.astype(BF16)
        for peer in range(peers):
            send_ref[peer * 8 : peer * 8 + 8, block * 128 : (block + 1) * 128] = tile


def decode_kernel(
    rows, peers, here, lat_ref, win_ref, w1_ref, b1_ref, dec_ref, res_ref, spread_out, shifted, weight, bias, act, taps
):
    t = here[0]
    slab_height = 2 * rows
    first_row = here[1] * slab_height
    count = rows + 2
    per = count // 2
    outs = w1_ref.shape[0] // 9
    lane = iota((1, 128), 1)
    all_out = peers * outs

    def load_weights(base, at):
        side = pltpu.roll(win_ref[pl.ds(pl.multiple_of(base + STAT, 16), 32), :].astype(F32), 64, 1)
        weight[at : at + outs, :128] = win_ref[pl.ds(pl.multiple_of(base + WROW, 16), 32), :]
        weight[at : at + outs, 128:] = jnp.where(lane < 16, side, 0.0).astype(BF16)
        total = side[:, 16:17] + side[:, 17:18] + side[:, 18:19]
        bias[at : at + outs, :] = jnp.broadcast_to(total, (outs, 128))

    for peer in range(peers):
        load_weights(peer * BLOCK, peer * outs)
    load_weights(t * BLOCK, all_out)

    r = iota((128, 512), 0)
    c = iota((128, 512), 1)
    token = 4 * (r // 8) + r % 4
    hot = ((r // 4) % 2 == c // 256) & (c % 128 == 2 * token + (c // 128) % 2)
    hot = hot.astype(F32).astype(BF16)
    spread_out[...] = lax.dot_general(lat_ref[...], hot, (((0,), (0,)), ((), ())), preferred_element_type=F32)
    for i in range(count):
        for a in range(2):
            at = (i % per) * 64 + a * 32
            base = (i // per) * 256
            pix = spread_out[at : at + 16, base : base + 128] + spread_out[at + 16 : at + 32, base + 128 : base + 256]
            row = (2 * i + a) * 48
            shifted[row : row + 16, :] = jnp.where(lane == 0, 0.0, pltpu.roll(pix, 1, 1)).astype(BF16)
            shifted[row + 16 : row + 32, :] = pix.astype(BF16)
            shifted[row + 32 : row + 48, :] = jnp.where(lane == 127, 0.0, pltpu.roll(pix, 127, 1)).astype(BF16)

    def finish(y):
        global_row = lax.rem(first_row + y, WPIX)
        up = global_row != 0
        down = global_row != WPIX - 1
        sums = taps[y + 1, 96:192, :]
        sums = sums + jnp.where(up, taps[y, 0:96, :], 0.0)
        sums = sums + jnp.where(down, taps[y + 2, 192:288, :], 0.0)
        total = sums[32:64, :] + b1_ref[...]
        total = total + jnp.where(lane == 0, 0.0, pltpu.roll(sums[0:32, :], 1, 1))
        total = total + jnp.where(lane == 127, 0.0, pltpu.roll(sums[64:96, :], 127, 1))
        res_ref[y] = total.astype(BF16)

    def pair(m, carry):
        parts = []
        for n in range(2):
            q = 2 * m + n
            global_row = lax.rem(first_row - 1 + q + WPIX, WPIX)
            block = shifted[pl.ds(pl.multiple_of(q * 48, 16), 144), :]
            up = jnp.where(global_row != 0, block[:48, :], jnp.zeros((48, 128), BF16))
            down = jnp.where(global_row != WPIX - 1, block[96:, :], jnp.zeros((48, 128), BF16))
            parts.append(jnp.concatenate([up, block[48:96, :], down], axis=0))
        right = jnp.concatenate(parts, axis=1)
        feat = jnp.dot(weight[:, :144], right, preferred_element_type=F32)
        both = jnp.concatenate([bias[...], bias[...]], axis=1)
        feat = (feat + both).astype(BF16)

        @pl.when(m > 0)
        def _():
            dec_ref[2 * m - 1] = feat[all_out:, :128]

        @pl.when(m < count - 2)
        def _():
            dec_ref[2 * m] = feat[all_out:, 128:]

        value = feat[:all_out, :].astype(F32)
        halved = 0.5 * value
        act[...] = (halved + halved * jnp.tanh(halved)).astype(BF16)
        tap = jnp.dot(w1_ref[...], act[...], preferred_element_type=F32)
        taps[2 * m] = tap[:, :128]
        taps[2 * m + 1] = tap[:, 128:]

        @pl.when(m > 0)
        def _():
            finish(2 * m - 2)
            finish(2 * m - 1)

        return carry

    lax.fori_loop(0, rows + 1, pair, 0)


def vmem():
    return pl.BlockSpec(memory_space=pltpu.VMEM)


def smem():
    return pl.BlockSpec(memory_space=pltpu.SMEM)


def call(body, inputs, kinds, out_shape, scratch, flops, bytes_accessed, limit):
    return pl.pallas_call(
        body,
        out_shape=out_shape,
        in_specs=[smem() if k == "s" else vmem() for k in kinds],
        out_specs=jax.tree.map(lambda _: vmem(), out_shape),
        scratch_shapes=scratch,
        compiler_params=pltpu.CompilerParams(vmem_limit_bytes=limit << 20),
        cost_estimate=pl.CostEstimate(flops=flops, bytes_accessed=bytes_accessed, transcendentals=0),
    )(*inputs)


def shards(
    hidden,
    modulation,
    final_weight,
    noisy,
    step_index,
    slab_table,
    conv_in_weight,
    conv_in_bias,
    conv1_weight,
    conv1_bias,
):
    peers = lax.axis_size("tensor")
    slabs = lax.axis_size("wide")
    t = lax.axis_index("tensor")
    w = lax.axis_index("wide")
    here = jnp.stack([t, w]).astype(jnp.int32)
    rows = slab_table.shape[0]
    feats = hidden.shape[1]
    outs = conv_in_weight.shape[1]
    sds = jax.ShapeDtypeStruct

    send, noisy_mine = call(
        functools.partial(project_kernel, rows, peers),
        (here, hidden.T, modulation, final_weight.T, conv_in_weight.T, conv_in_bias.reshape(1, -1), noisy.T),
        "svvvvvv",
        (sds((peers * BLOCK, 128), BF16), sds((2 * SR, 128), F32)),
        [pltpu.VMEM((rows * GRID, 128), F32), pltpu.VMEM((rows * GRID, 64), F32)],
        10**9,
        2 * 10**6,
        16,
    )
    recv = lax.all_to_all(send, "tensor", split_axis=0, concat_axis=0, tiled=True)
    routed = call(
        functools.partial(clean_kernel, rows, peers, slabs, feats),
        (step_index, slab_table, recv, noisy_mine),
        "ssvv",
        sds((slabs * 8, 128), BF16),
        [],
        10**7,
        10**6,
        8,
    )
    landed = lax.all_to_all(routed, "wide", split_axis=0, concat_axis=0, tiled=True)
    width = 128 * (((rows + 2) // 2 + 1) // 2)
    copies = call(
        functools.partial(pick_kernel, rows, peers, slabs),
        (here, slab_table, landed),
        "ssv",
        sds((peers * 8, width), BF16),
        [pltpu.VMEM((slabs * 8, 128), F32)],
        10**6,
        10**6,
        8,
    )
    latents = lax.all_to_all(copies, "tensor", split_axis=0, concat_axis=0, tiled=True)
    own = lax.dynamic_slice_in_dim(conv1_weight, t * outs, outs, 2)
    w1 = own.transpose(0, 2, 1).reshape(9 * outs, -1)
    b1 = jnp.broadcast_to(lax.dynamic_slice_in_dim(conv1_bias, t * outs, outs, 0)[:, None], (outs, 128))
    channels = w1.shape[1]
    return call(
        functools.partial(decode_kernel, rows, peers),
        (here, latents, recv, w1, b1),
        "svvvv",
        (sds((2 * rows, outs, WPIX), BF16), sds((2 * rows, outs, WPIX), BF16)),
        [
            pltpu.VMEM((width // 128 * 128, 512), F32),
            pltpu.VMEM((2 * (rows + 2) * 48, 128), BF16),
            pltpu.VMEM((channels + outs, 256), BF16),
            pltpu.VMEM((channels + outs, 128), F32),
            pltpu.VMEM((channels, 256), BF16),
            pltpu.VMEM((2 * rows + 2, 9 * outs, 128), F32),
        ],
        6 * 10**9,
        3 * 10**6,
        24,
    )


def solution(mesh):
    return jax.shard_map(
        shards,
        mesh=mesh,
        in_specs=(
            P("wide", "tensor"),
            P(None, "tensor"),
            P("tensor", None),
            P("wide", None),
            P(),
            P("wide"),
            P(None, "tensor"),
            P("tensor"),
            P(),
            P(),
        ),
        out_specs=(P("wide", "tensor", None), P("wide", "tensor", None)),
        check_vma=False,
    )
```

```python
import functools

import jax
import jax.numpy as jnp
from jax import lax
from jax.experimental import pallas as pl
from jax.experimental.pallas import tpu as pltpu
from jax.sharding import PartitionSpec as P

D = 3072
LC = 16
GRID = 64
STEPS = 28
WPIX = 128
shift_value = 3.0
norm_eps = 1e-06

F32 = jnp.float32
BF16 = jnp.bfloat16

SR = 24
STAT = 2 * SR
WROW = STAT + 16
BLOCK = WROW + 32


def iota(shape, dim):
    return lax.broadcasted_iota(jnp.int32, shape, dim)


def thirds(value):
    first = value.astype(BF16).astype(F32)
    rest = value - first
    second = rest.astype(BF16).astype(F32)
    return (first, second, (rest - second).astype(BF16).astype(F32))


def to_column(row):
    n = row.shape[1]
    return jnp.sum(jnp.where(iota((n, n), 0) == iota((n, n), 1), row, 0.0), axis=1, keepdims=True)


def to_row(column):
    n = column.shape[0]
    return jnp.sum(jnp.where(iota((n, n), 0) == iota((n, n), 1), column, 0.0), axis=0, keepdims=True)


def project_kernel(rows, peers, here, h_hbm, noisy_hbm, *rest):
    small = rest[:4]
    send_ref, side_ref, h_ref, noisy_ref, mod_ref, w_ref, win_ref, bin_ref, sums, drawn, sems = rest[4:]
    moves = zip((h_hbm, *small, noisy_hbm), (h_ref, mod_ref, w_ref, win_ref, bin_ref, noisy_ref))
    copies = [pltpu.make_async_copy(src, dst, sems.at[n]) for n, (src, dst) in enumerate(moves)]
    for copy in copies:
        copy.start()
    for copy in copies[1:5]:
        copy.wait()
    per = GRID // peers
    feats = h_ref.shape[0]
    weight = w_ref[...].astype(F32)
    scaled = (1.0 + mod_ref[1:2, :]) * weight
    colsum = jnp.sum(scaled, axis=1, keepdims=True)
    shifted = jnp.sum(mod_ref[0:1, :] * weight, axis=1, keepdims=True)
    left = jnp.concatenate(thirds(scaled - colsum / feats), axis=0).astype(BF16)
    lane = iota((1, 128), 1)
    low = lane < 64
    step = 256
    copies[0].wait()
    for at in range(0, h_ref.shape[1], step):
        hid = h_ref[:, at : at + step]
        prod = jnp.dot(left, hid, preferred_element_type=F32)
        wide = hid.astype(F32)
        pieces = thirds(jnp.sum(wide, axis=0, keepdims=True)) + thirds(jnp.sum(wide * wide, axis=0, keepdims=True))
        stats = [jnp.broadcast_to(p, (4, step)) for p in pieces] + [jnp.zeros((40, step), F32)]
        both = jnp.concatenate([prod[:64, :] + prod[64:128, :] + prod[128:, :]] + stats, axis=0)
        sums[at : at + step, :] = jnp.transpose(both)
    win = win_ref[...].astype(F32)
    outs = win.shape[0]
    rest_w = jnp.concatenate([win[:, 128:], jnp.zeros((outs, 128 - (win.shape[1] - 128)), F32)], axis=1)
    bias = jnp.zeros((outs, 128), F32)
    for n, piece in enumerate(thirds(to_column(bin_ref[...]))):
        bias = jnp.where(lane == n, piece, bias)
    pad = jnp.zeros((1, 64), F32)
    lines = thirds(to_row(colsum)) + thirds(to_row(shifted))
    lower = jnp.concatenate([jnp.concatenate([v, pad], axis=1) for v in lines] + [jnp.zeros((2, 128), F32)], axis=0)
    upper = jnp.zeros((8, 128), F32)
    for g in range(outs // 8):
        upper = upper + pltpu.roll(bias[8 * g : 8 * g + 8, :], 72 + 4 * g, 1)
        lower = lower + pltpu.roll(rest_w[8 * g : 8 * g + 8, :], 64 + 16 * g, 1)
    main_w = win_ref[:, :128]
    fill = [jnp.zeros((SR - rows, 128), F32)] if rows < SR else []
    for peer in range(peers):
        base = peer * BLOCK
        stat = jnp.zeros((SR, 128), F32)
        halves = []
        for dk in range(per):
            val = sums[pl.ds(peer * per + dk, rows, stride=GRID), :]
            val = jnp.concatenate([val] + fill, axis=0) if fill else val
            turned = pltpu.roll(val, 64, 1)
            stat = jnp.where((lane % 4 == dk) & (lane < 24), turned, stat)
            halves.append(val if dk % 2 == 0 else turned)
        for half in range(per // 2):
            joined = jnp.where(low, halves[2 * half], halves[2 * half + 1])
            send_ref[base + half * SR : base + (half + 1) * SR, :] = joined.astype(BF16)
        tile = upper
        for g in range(SR // 8):
            tile = tile + (pltpu.roll(stat[8 * g : 8 * g + 8, :], 24 * g, 1) if g else stat[:8, :])
        send_ref[base + STAT : base + STAT + 16, :] = jnp.concatenate([tile, lower], axis=0).astype(BF16)
        send_ref[base + WROW : base + WROW + 32, :] = main_w
    owner = jnp.full((8, 128), -9, jnp.int32)
    for j in range(rows):
        owner = jnp.where((lane % SR == j) & (lane < 4 * SR), here[3 + j], owner)
    frac = (jnp.zeros((8, 128), F32) + here[2].astype(F32)) / STEPS
    sigma = shift_value * frac / (1.0 + (shift_value - 1.0) * frac)
    side_ref[2 * SR : 2 * SR + 8, :] = owner.astype(F32)
    side_ref[2 * SR + 8 : 2 * SR + 16, :] = sigma
    copies[5].wait()
    for at in range(0, h_ref.shape[1], step):
        drawn[at : at + step, :] = jnp.transpose(noisy_ref[:, at : at + step])
    mine = here[0] * per
    for half in range(per // 2):
        one = drawn[pl.ds(mine + 2 * half, rows, stride=GRID), :]
        two = drawn[pl.ds(mine + 2 * half + 1, rows, stride=GRID), :]
        both = jnp.concatenate([one, two], axis=1)
        side_ref[half * SR : (half + 1) * SR, :] = jnp.concatenate([both] + fill, axis=0) if fill else both


def spread(tile, at, low):
    parts = []
    for half in range(2):
        a = tile[:, at + 2 * half : at + 2 * half + 1]
        b = tile[:, at + 2 * half + 1 : at + 2 * half + 2]
        parts.append(jnp.where(low, a, b))
    return jnp.concatenate(parts, axis=0)


def clean_kernel(rows, peers, slabs, feats, recv_ref, side_ref, send_ref):
    lane = iota((1, 128), 1)
    low = lane < 64
    total = jnp.zeros((2 * SR, 128), F32)
    means = []
    columns = []
    sums = jnp.zeros((SR, 128), F32)
    shifted = jnp.zeros((1, 128), F32)
    for peer in range(peers):
        base = peer * BLOCK
        total = total + recv_ref[base : base + 2 * SR, :].astype(F32)
        tile = recv_ref[base + STAT : base + STAT + 16, :].astype(F32)
        upper = tile[:8, :]
        lines = tile[8:, :]
        stat = jnp.concatenate([upper, pltpu.roll(upper, 104, 1), pltpu.roll(upper, 80, 1)], axis=0)
        stat = stat + pltpu.roll(stat, 124, 1) + pltpu.roll(stat, 120, 1)
        sums = sums + stat
        means.append(stat / feats)
        cs = jnp.where(low, lines[0:1, :] + lines[1:2, :] + lines[2:3, :], 0.0)
        columns.append(cs + pltpu.roll(cs, 64, 1))
        sw = jnp.where(low, lines[3:4, :] + lines[4:5, :] + lines[5:6, :], 0.0)
        shifted = shifted + sw + pltpu.roll(sw, 64, 1)
    mean = sums / (feats * peers)
    for m, cs in zip(means, columns):
        total = total + spread(m - mean, 0, low) * cs
    square = pltpu.roll(mean, 116, 1)
    rstd = 1.0 / jnp.sqrt(square - mean * mean + norm_eps)
    velocity = total * spread(rstd, 0, low) + shifted
    sigma = side_ref[2 * SR + 8 : 2 * SR + 9, :]
    clean = (side_ref[: 2 * SR, :] - sigma * velocity).astype(BF16).astype(F32)
    held = jnp.concatenate([clean, pltpu.roll(clean, 64, 1), jnp.zeros((128 - 4 * SR, 128), F32)], axis=0).astype(BF16)
    owner = side_ref[2 * SR : 2 * SR + 1, :].astype(jnp.int32)
    shape = (slabs * 8, 128)
    row = iota(shape, 0)
    col = iota(shape, 1)
    slab = row // 8
    upper = row % 8 < 4
    dk = row % 4
    turned = col // (2 * SR)
    half = (col // SR) % 2
    j = col % SR
    right_half = half == dk // 2
    target = jnp.where(upper, owner, jnp.where(j == 0, owner - 1, -9))
    own = target == slab
    take_low = (right_half & (turned == dk % 2) & own).astype(F32).astype(BF16)
    above = upper & (j == rows - 1) & (owner + 1 == slab) & (owner >= 0)
    take_high = (right_half & (turned == 1 - dk % 2) & above).astype(F32).astype(BF16)
    left = jnp.dot(take_low, held, preferred_element_type=F32)
    right = jnp.dot(take_high, held, preferred_element_type=F32)
    send_ref[...] = jnp.where(low, left, right).astype(BF16)


def pick_kernel(rows, peers, slabs, here, recv_ref, send_ref, wide):
    wide[...] = recv_ref[...].astype(F32)
    lane = iota((8, 128), 1)
    low = lane < 64
    top = iota((8, 128), 0) < 4
    count = rows + 2
    per = count // 2

    def source(j):
        return lax.rem(2 * here[1] - here[3 + j] + 2 * slabs, slabs)

    def piece(i, at_low, at_top):
        if i == 0:
            x, is_low, is_top = (lax.rem(source(rows - 1) - 1 + slabs, slabs), False, True)
        elif i == count - 1:
            x, is_low, is_top = (lax.rem(source(0) + 1, slabs), True, False)
        else:
            x, is_low, is_top = (source(i - 1), True, True)
        tile = wide[pl.ds(pl.multiple_of(x * 8, 8), 8), :]
        if is_low != at_low:
            tile = pltpu.roll(tile, 64, 1)
        if is_top != at_top:
            tile = pltpu.roll(tile, 4, 0)
        return tile

    for block in range((per + 1) // 2):
        quarters = []
        for at_top in (True, False):
            for at_low in (True, False):
                n = 2 * block + (0 if at_low else 1)
                if n < per:
                    quarters.append(piece(n + (0 if at_top else per), at_low, at_top))
                else:
                    quarters.append(jnp.zeros((8, 128), F32))
        tile = jnp.where(top, jnp.where(low, quarters[0], quarters[1]), jnp.where(low, quarters[2], quarters[3]))
        tile = tile.astype(BF16)
        for peer in range(peers):
            send_ref[peer * 8 : peer * 8 + 8, block * 128 : (block + 1) * 128] = tile


def gather_kernel(peers, here, recv_ref, weight, bias):
    lane = iota((1, 128), 1)
    outs = weight.shape[0] // (peers + 1)

    def load(base, at):
        tile = recv_ref[pl.ds(pl.multiple_of(base + STAT, 16), 16), :].astype(F32)
        groups = range(outs // 8)
        side = jnp.concatenate([pltpu.roll(tile[8:, :], 64 - 16 * g, 1) for g in groups], axis=0)
        turned = jnp.concatenate([pltpu.roll(tile[:8, :], 56 - 4 * g, 1) for g in groups], axis=0)
        weight[at : at + outs, :128] = recv_ref[pl.ds(pl.multiple_of(base + WROW, 16), 32), :]
        weight[at : at + outs, 128:] = side[:, :16].astype(BF16)
        total = turned[:, 0:1] + turned[:, 1:2] + turned[:, 2:3]
        bias[at : at + outs, :] = jnp.broadcast_to(total, (outs, 128))

    for peer in range(peers):
        load(peer * BLOCK, peer * outs)
    load(here[0] * BLOCK, peers * outs)


def decode_kernel(rows, here, lat_ref, weight, bias, w1_ref, b1_ref, dec_ref, res_ref, spread_out, shifted, act, act2, taps):
    slab_height = 2 * rows
    first_row = here[1] * slab_height
    count = rows + 2
    per = count // 2
    outs = w1_ref.shape[0] // 9
    lane = iota((1, 128), 1)
    all_out = w1_ref.shape[1]

    r = iota((128, 512), 0)
    c = iota((128, 512), 1)
    token = 4 * (r // 8) + r % 4
    hot = ((r // 4) % 2 == c // 256) & (c % 128 == 2 * token + (c // 128) % 2)
    hot = hot.astype(F32).astype(BF16)
    spread_out[...] = lax.dot_general(lat_ref[...], hot, (((0,), (0,)), ((), ())), preferred_element_type=F32)
    for i in range(count):
        for a in range(2):
            at = (i % per) * 64 + a * 32
            base = (i // per) * 256
            pix = spread_out[at : at + 16, base : base + 128] + spread_out[at + 16 : at + 32, base + 128 : base + 256]
            row = (2 * i + a) * 48
            shifted[row : row + 16, :] = jnp.where(lane == 0, 0.0, pltpu.roll(pix, 1, 1)).astype(BF16)
            shifted[row + 16 : row + 32, :] = pix.astype(BF16)
            shifted[row + 32 : row + 48, :] = jnp.where(lane == 127, 0.0, pltpu.roll(pix, 127, 1)).astype(BF16)

    def features(m, buf):
        parts = []
        for n in range(2):
            q = 2 * m + n
            global_row = lax.rem(first_row - 1 + q + WPIX, WPIX)
            block = shifted[pl.ds(pl.multiple_of(q * 48, 16), 144), :]
            up = jnp.where(global_row != 0, block[:48, :], jnp.zeros((48, 128), BF16))
            down = jnp.where(global_row != WPIX - 1, block[96:, :], jnp.zeros((48, 128), BF16))
            parts.append(jnp.concatenate([up, block[48:96, :], down], axis=0))
        right = jnp.concatenate(parts, axis=1)
        feat = jnp.dot(weight[...], right, preferred_element_type=F32)
        both = jnp.concatenate([bias[...], bias[...]], axis=1)
        feat = (feat + both).astype(BF16)
        dec_ref[jnp.minimum(2 * m, slab_height - 1)] = feat[all_out:, 128:]
        dec_ref[jnp.abs(2 * m - 1)] = feat[all_out:, :128]
        value = feat[:all_out, :].astype(F32)
        halved = 0.5 * value
        buf[...] = (halved + halved * jnp.tanh(halved)).astype(BF16)

    def multiply(m, buf):
        tap = jnp.dot(w1_ref[...], buf[...], preferred_element_type=F32)
        taps[2 * m] = tap[:, :128]
        taps[2 * m + 1] = tap[:, 128:]

    def finish(m):
        for y in (2 * m - 2, 2 * m - 1):
            global_row = lax.rem(first_row + y, WPIX)
            sums = taps[y + 1, 3 * outs : 6 * outs, :]
            sums = sums + jnp.where(global_row != 0, taps[y, 0 : 3 * outs, :], 0.0)
            sums = sums + jnp.where(global_row != WPIX - 1, taps[y + 2, 6 * outs :, :], 0.0)
            total = sums[outs : 2 * outs, :] + b1_ref[...]
            total = total + jnp.where(lane == 0, 0.0, pltpu.roll(sums[0:outs, :], 1, 1))
            total = total + jnp.where(lane == 127, 0.0, pltpu.roll(sums[2 * outs :, :], 127, 1))
            res_ref[y] = total.astype(BF16)

    features(0, act)
    taps[0:4] = jnp.zeros((4, 9 * outs, 128), F32)

    def double(step, carry):
        for n, (now, before) in enumerate(((act2, act), (act, act2))):
            m = 2 * step + 1 + n
            features(m, now)
            multiply(m - 1, before)
            finish(jnp.maximum(m - 2, 1))
        return carry

    lax.fori_loop(0, rows // 2, double, 0)
    multiply(rows, act)
    finish(rows - 1)
    finish(rows)


SPACES = {"s": pltpu.SMEM, "v": pltpu.VMEM, "h": pltpu.HBM}


def call(body, inputs, kinds, out_shape, scratch, flops, bytes_accessed, limit):
    return pl.pallas_call(
        body,
        out_shape=out_shape,
        in_specs=[pl.BlockSpec(memory_space=SPACES[k]) for k in kinds],
        out_specs=jax.tree.map(lambda _: pl.BlockSpec(memory_space=pltpu.VMEM), out_shape),
        scratch_shapes=scratch,
        compiler_params=pltpu.CompilerParams(vmem_limit_bytes=limit << 20),
        cost_estimate=pl.CostEstimate(flops=flops, bytes_accessed=bytes_accessed, transcendentals=0),
    )(*inputs)


def decode_call(rows, here, latents, weight, bias, w1, b1):
    width = latents.shape[1]
    outs = w1.shape[0] // 9
    channels = w1.shape[1]
    shape = jax.ShapeDtypeStruct((2 * rows, outs, WPIX), BF16)
    return call(
        functools.partial(decode_kernel, rows),
        (here, latents, weight, bias, w1, b1),
        "svvvvv",
        (shape, shape),
        [
            pltpu.VMEM((width, 512), F32),
            pltpu.VMEM((2 * (rows + 2) * 48, 128), BF16),
            pltpu.VMEM((channels, 256), BF16),
            pltpu.VMEM((channels, 256), BF16),
            pltpu.VMEM((2 * rows + 2, 9 * outs, 128), F32),
        ],
        6 * 10**9,
        3 * 10**6,
        24,
    )


def gather_call(here, recv, peers, outs):
    sds = jax.ShapeDtypeStruct
    many = (peers + 1) * outs
    return call(
        functools.partial(gather_kernel, peers),
        (here, recv),
        "sv",
        (sds((many, 144), BF16), sds((many, 128), F32)),
        [],
        10**6,
        10**6,
        8,
    )


def shards(
    hidden,
    modulation,
    final_weight,
    noisy,
    step_index,
    slab_table,
    conv_in_weight,
    conv_in_bias,
    conv1_weight,
    conv1_bias,
):
    peers = lax.axis_size("tensor")
    slabs = lax.axis_size("wide")
    t = lax.axis_index("tensor")
    w = lax.axis_index("wide")
    here = jnp.concatenate([jnp.stack([t, w]).astype(jnp.int32), step_index, slab_table])
    rows = slab_table.shape[0]
    tokens, feats = hidden.shape
    outs = conv_in_weight.shape[1]
    sds = jax.ShapeDtypeStruct
    large = (hidden.T, noisy.T)
    small = (modulation, final_weight.T, conv_in_weight.T, conv_in_bias.reshape(1, -1))

    send, side = call(
        functools.partial(project_kernel, rows, peers),
        (here, hidden.T, noisy.T, *small),
        "shhhhhh",
        (sds((peers * BLOCK, 128), BF16), sds((2 * SR + 16, 128), F32)),
        [pltpu.VMEM(x.shape, x.dtype) for x in large + small]
        + [pltpu.VMEM((tokens, 128), F32), pltpu.VMEM((tokens, noisy.shape[1]), F32), pltpu.SemaphoreType.DMA((6,))],
        10**9,
        2 * 10**6,
        60,
    )
    recv = lax.all_to_all(send, "tensor", split_axis=0, concat_axis=0, tiled=True)
    routed = call(
        functools.partial(clean_kernel, rows, peers, slabs, feats),
        (recv, side),
        "vv",
        sds((slabs * 8, 128), BF16),
        [],
        10**7,
        10**6,
        8,
    )
    landed = lax.all_to_all(routed, "wide", split_axis=0, concat_axis=0, tiled=True)
    width = 128 * (((rows + 2) // 2 + 1) // 2)
    copies = call(
        functools.partial(pick_kernel, rows, peers, slabs),
        (here, landed),
        "sv",
        sds((peers * 8, width), BF16),
        [pltpu.VMEM((slabs * 8, 128), F32)],
        10**6,
        10**6,
        8,
    )
    latents = lax.all_to_all(copies, "tensor", split_axis=0, concat_axis=0, tiled=True)
    own = lax.dynamic_slice_in_dim(conv1_weight, t * outs, outs, 2)
    w1 = own.transpose(0, 2, 1).reshape(9 * outs, -1)
    b1 = jnp.broadcast_to(lax.dynamic_slice_in_dim(conv1_bias, t * outs, outs, 0)[:, None], (outs, 128))
    weight, bias = gather_call(here, recv, peers, outs)
    return decode_call(rows, here, latents, weight, bias, w1, b1)


def solution(mesh):
    return jax.shard_map(
        shards,
        mesh=mesh,
        in_specs=(
            P("wide", "tensor"),
            P(None, "tensor"),
            P("tensor", None),
            P("wide", None),
            P(),
            P("wide"),
            P(None, "tensor"),
            P("tensor"),
            P(),
            P(),
        ),
        out_specs=(P("wide", "tensor", None), P("wide", "tensor", None)),
        check_vma=False,
    )
```

```python
import functools

import jax
import jax.numpy as jnp
from jax import lax
from jax.experimental import pallas as pl
from jax.experimental.pallas import tpu as pltpu
from jax.sharding import PartitionSpec as P

D = 3072
LC = 16
GRID = 64
STEPS = 28
WPIX = 128
shift_value = 3.0
norm_eps = 1e-06

F32 = jnp.float32
BF16 = jnp.bfloat16

SR = 24
STAT = 2 * SR
WROW = STAT + 16
BLOCK = WROW + 32


def iota(shape, dim):
    return lax.broadcasted_iota(jnp.int32, shape, dim)


def thirds(value):
    first = value.astype(BF16).astype(F32)
    rest = value - first
    second = rest.astype(BF16).astype(F32)
    return (first, second, (rest - second).astype(BF16).astype(F32))


def to_column(row):
    n = row.shape[1]
    return jnp.sum(jnp.where(iota((n, n), 0) == iota((n, n), 1), row, 0.0), axis=1, keepdims=True)


def to_row(column):
    n = column.shape[0]
    return jnp.sum(jnp.where(iota((n, n), 0) == iota((n, n), 1), column, 0.0), axis=0, keepdims=True)


def project_kernel(rows, peers, h_hbm, *rest):
    small = rest[:4]
    send_ref, h_ref, mod_ref, w_ref, win_ref, bin_ref, sums, sems = rest[4:]
    moves = list(zip(small, (mod_ref, w_ref, win_ref, bin_ref)))
    moves.append((h_hbm, h_ref))
    copies = [pltpu.make_async_copy(src, dst, sems.at[n]) for n, (src, dst) in enumerate(moves)]
    for copy in copies:
        copy.start()
    for copy in copies[:4]:
        copy.wait()
    per = GRID // peers
    feats = h_ref.shape[0]
    weight = w_ref[...].astype(F32)
    scaled = (1.0 + mod_ref[1:2, :]) * weight
    colsum = jnp.sum(scaled, axis=1, keepdims=True)
    shifted = jnp.sum(mod_ref[0:1, :] * weight, axis=1, keepdims=True)
    left = jnp.concatenate(thirds(scaled - colsum / feats), axis=0).astype(BF16)
    lane = iota((1, 128), 1)
    low = lane < 64
    step = 256
    copies[4].wait()
    for at in range(0, h_ref.shape[1], step):
        hid = h_ref[:, at : at + step]
        prod = jnp.dot(left, hid, preferred_element_type=F32)
        wide = hid.astype(F32)
        pieces = thirds(jnp.sum(wide, axis=0, keepdims=True)) + thirds(jnp.sum(wide * wide, axis=0, keepdims=True))
        stats = [jnp.broadcast_to(p, (4, step)) for p in pieces] + [jnp.zeros((40, step), F32)]
        both = jnp.concatenate([prod[:64, :] + prod[64:128, :] + prod[128:, :]] + stats, axis=0)
        sums[at : at + step, :] = jnp.transpose(both)
    win = win_ref[...].astype(F32)
    outs = win.shape[0]
    rest_w = jnp.concatenate([win[:, 128:], jnp.zeros((outs, 128 - (win.shape[1] - 128)), F32)], axis=1)
    bias = jnp.zeros((outs, 128), F32)
    for n, piece in enumerate(thirds(to_column(bin_ref[...]))):
        bias = jnp.where(lane == n, piece, bias)
    pad = jnp.zeros((1, 64), F32)
    lines = thirds(to_row(colsum)) + thirds(to_row(shifted))
    lower = jnp.concatenate([jnp.concatenate([v, pad], axis=1) for v in lines] + [jnp.zeros((2, 128), F32)], axis=0)
    upper = jnp.zeros((8, 128), F32)
    for g in range(outs // 8):
        upper = upper + pltpu.roll(bias[8 * g : 8 * g + 8, :], 72 + 4 * g, 1)
        lower = lower + pltpu.roll(rest_w[8 * g : 8 * g + 8, :], 64 + 16 * g, 1)
    main_w = win_ref[:, :128]
    fill = [jnp.zeros((SR - rows, 128), F32)] if rows < SR else []
    for peer in range(peers):
        base = peer * BLOCK
        stat = jnp.zeros((SR, 128), F32)
        halves = []
        for dk in range(per):
            val = sums[pl.ds(peer * per + dk, rows, stride=GRID), :]
            val = jnp.concatenate([val] + fill, axis=0) if fill else val
            turned = pltpu.roll(val, 64, 1)
            stat = jnp.where((lane % 4 == dk) & (lane < 24), turned, stat)
            halves.append(val if dk % 2 == 0 else turned)
        for half in range(per // 2):
            joined = jnp.where(low, halves[2 * half], halves[2 * half + 1])
            send_ref[base + half * SR : base + (half + 1) * SR, :] = joined.astype(BF16)
        tile = upper
        for g in range(SR // 8):
            tile = tile + (pltpu.roll(stat[8 * g : 8 * g + 8, :], 24 * g, 1) if g else stat[:8, :])
        send_ref[base + STAT : base + STAT + 16, :] = jnp.concatenate([tile, lower], axis=0).astype(BF16)
        send_ref[base + WROW : base + WROW + 32, :] = main_w


def side_kernel(rows, peers, here, noisy_ref, side_ref, drawn):
    per = GRID // peers
    lane = iota((1, 128), 1)
    fill = [jnp.zeros((SR - rows, 128), F32)] if rows < SR else []
    owner = jnp.full((8, 128), -9, jnp.int32)
    for j in range(rows):
        owner = jnp.where((lane % SR == j) & (lane < 4 * SR), here[3 + j], owner)
    frac = (jnp.zeros((8, 128), F32) + here[2].astype(F32)) / STEPS
    sigma = shift_value * frac / (1.0 + (shift_value - 1.0) * frac)
    side_ref[2 * SR : 2 * SR + 8, :] = owner.astype(F32)
    side_ref[2 * SR + 8 : 2 * SR + 16, :] = sigma
    for at in range(0, noisy_ref.shape[1], 256):
        drawn[at : at + 256, :] = jnp.transpose(noisy_ref[:, at : at + 256])
    mine = here[0] * per
    for half in range(per // 2):
        one = drawn[pl.ds(mine + 2 * half, rows, stride=GRID), :]
        two = drawn[pl.ds(mine + 2 * half + 1, rows, stride=GRID), :]
        both = jnp.concatenate([one, two], axis=1)
        side_ref[half * SR : (half + 1) * SR, :] = jnp.concatenate([both] + fill, axis=0) if fill else both


def spread(tile, at, low):
    parts = []
    for half in range(2):
        a = tile[:, at + 2 * half : at + 2 * half + 1]
        b = tile[:, at + 2 * half + 1 : at + 2 * half + 2]
        parts.append(jnp.where(low, a, b))
    return jnp.concatenate(parts, axis=0)


def clean_kernel(rows, peers, slabs, feats, recv_ref, side_ref, send_ref):
    lane = iota((1, 128), 1)
    low = lane < 64
    total = jnp.zeros((2 * SR, 128), F32)
    means = []
    columns = []
    sums = jnp.zeros((SR, 128), F32)
    shifted = jnp.zeros((1, 128), F32)
    for peer in range(peers):
        base = peer * BLOCK
        total = total + recv_ref[base : base + 2 * SR, :].astype(F32)
        tile = recv_ref[base + STAT : base + STAT + 16, :].astype(F32)
        upper = tile[:8, :]
        lines = tile[8:, :]
        stat = jnp.concatenate([upper, pltpu.roll(upper, 104, 1), pltpu.roll(upper, 80, 1)], axis=0)
        stat = stat + pltpu.roll(stat, 124, 1) + pltpu.roll(stat, 120, 1)
        sums = sums + stat
        means.append(stat / feats)
        cs = jnp.where(low, lines[0:1, :] + lines[1:2, :] + lines[2:3, :], 0.0)
        columns.append(cs + pltpu.roll(cs, 64, 1))
        sw = jnp.where(low, lines[3:4, :] + lines[4:5, :] + lines[5:6, :], 0.0)
        shifted = shifted + sw + pltpu.roll(sw, 64, 1)
    mean = sums / (feats * peers)
    for m, cs in zip(means, columns):
        total = total + spread(m - mean, 0, low) * cs
    square = pltpu.roll(mean, 116, 1)
    rstd = 1.0 / jnp.sqrt(square - mean * mean + norm_eps)
    velocity = total * spread(rstd, 0, low) + shifted
    sigma = side_ref[2 * SR + 8 : 2 * SR + 9, :]
    clean = (side_ref[: 2 * SR, :] - sigma * velocity).astype(BF16).astype(F32)
    held = jnp.concatenate([clean, pltpu.roll(clean, 64, 1), jnp.zeros((128 - 4 * SR, 128), F32)], axis=0).astype(BF16)
    owner = side_ref[2 * SR : 2 * SR + 1, :].astype(jnp.int32)
    shape = (slabs * 8, 128)
    row = iota(shape, 0)
    col = iota(shape, 1)
    slab = row // 8
    upper = row % 8 < 4
    dk = row % 4
    turned = col // (2 * SR)
    half = (col // SR) % 2
    j = col % SR
    right_half = half == dk // 2
    target = jnp.where(upper, owner, jnp.where(j == 0, owner - 1, -9))
    own = target == slab
    take_low = (right_half & (turned == dk % 2) & own).astype(F32).astype(BF16)
    above = upper & (j == rows - 1) & (owner + 1 == slab) & (owner >= 0)
    take_high = (right_half & (turned == 1 - dk % 2) & above).astype(F32).astype(BF16)
    left = jnp.dot(take_low, held, preferred_element_type=F32)
    right = jnp.dot(take_high, held, preferred_element_type=F32)
    send_ref[...] = jnp.where(low, left, right).astype(BF16)


def pick_kernel(rows, peers, slabs, here, recv_ref, send_ref, wide):
    wide[...] = recv_ref[...].astype(F32)
    lane = iota((8, 128), 1)
    low = lane < 64
    top = iota((8, 128), 0) < 4
    count = rows + 2
    per = count // 2

    def source(j):
        return lax.rem(2 * here[1] - here[3 + j] + 2 * slabs, slabs)

    def piece(i, at_low, at_top):
        if i == 0:
            x, is_low, is_top = (lax.rem(source(rows - 1) - 1 + slabs, slabs), False, True)
        elif i == count - 1:
            x, is_low, is_top = (lax.rem(source(0) + 1, slabs), True, False)
        else:
            x, is_low, is_top = (source(i - 1), True, True)
        tile = wide[pl.ds(pl.multiple_of(x * 8, 8), 8), :]
        if is_low != at_low:
            tile = pltpu.roll(tile, 64, 1)
        if is_top != at_top:
            tile = pltpu.roll(tile, 4, 0)
        return tile

    for block in range((per + 1) // 2):
        quarters = []
        for at_top in (True, False):
            for at_low in (True, False):
                n = 2 * block + (0 if at_low else 1)
                if n < per:
                    quarters.append(piece(n + (0 if at_top else per), at_low, at_top))
                else:
                    quarters.append(jnp.zeros((8, 128), F32))
        tile = jnp.where(top, jnp.where(low, quarters[0], quarters[1]), jnp.where(low, quarters[2], quarters[3]))
        tile = tile.astype(BF16)
        for peer in range(peers):
            send_ref[peer * 8 : peer * 8 + 8, block * 128 : (block + 1) * 128] = tile


def gather_kernel(peers, here, recv_ref, weight, bias):
    lane = iota((1, 128), 1)
    outs = weight.shape[0] // (peers + 1)

    def load(base, at):
        tile = recv_ref[pl.ds(pl.multiple_of(base + STAT, 16), 16), :].astype(F32)
        groups = range(outs // 8)
        side = jnp.concatenate([pltpu.roll(tile[8:, :], 64 - 16 * g, 1) for g in groups], axis=0)
        turned = jnp.concatenate([pltpu.roll(tile[:8, :], 56 - 4 * g, 1) for g in groups], axis=0)
        weight[at : at + outs, :128] = recv_ref[pl.ds(pl.multiple_of(base + WROW, 16), 32), :]
        weight[at : at + outs, 128:] = side[:, :16].astype(BF16)
        total = turned[:, 0:1] + turned[:, 1:2] + turned[:, 2:3]
        bias[at : at + outs, :] = jnp.broadcast_to(total, (outs, 128))

    for peer in range(peers):
        load(peer * BLOCK, peer * outs)
    load(here[0] * BLOCK, peers * outs)


def decode_kernel(rows, here, lat_ref, weight, bias, w1_ref, b1_ref, dec_ref, res_ref, spread_out, shifted, act, act2, tap0, tap1, tap2, tap3):
    slab_height = 2 * rows
    first_row = here[1] * slab_height
    count = rows + 2
    per = count // 2
    outs = w1_ref.shape[0] // 9
    lane = iota((1, 128), 1)
    all_out = w1_ref.shape[1]

    r = iota((128, 512), 0)
    c = iota((128, 512), 1)
    token = 4 * (r // 8) + r % 4
    hot = ((r // 4) % 2 == c // 256) & (c % 128 == 2 * token + (c // 128) % 2)
    hot = hot.astype(F32).astype(BF16)
    spread_out[...] = lax.dot_general(lat_ref[...], hot, (((0,), (0,)), ((), ())), preferred_element_type=F32)
    for i in range(count):
        for a in range(2):
            at = (i % per) * 64 + a * 32
            base = (i // per) * 256
            pix = spread_out[at : at + 16, base : base + 128] + spread_out[at + 16 : at + 32, base + 128 : base + 256]
            row = (2 * i + a) * 48
            shifted[row : row + 16, :] = jnp.where(lane == 0, 0.0, pltpu.roll(pix, 1, 1)).astype(BF16)
            shifted[row + 16 : row + 32, :] = pix.astype(BF16)
            shifted[row + 32 : row + 48, :] = jnp.where(lane == 127, 0.0, pltpu.roll(pix, 127, 1)).astype(BF16)

    def features(m, buf):
        parts = []
        for n in range(2):
            q = 2 * m + n
            global_row = lax.rem(first_row - 1 + q + WPIX, WPIX)
            block = shifted[pl.ds(pl.multiple_of(q * 48, 16), 144), :]
            up = jnp.where(global_row != 0, block[:48, :], jnp.zeros((48, 128), BF16))
            down = jnp.where(global_row != WPIX - 1, block[96:, :], jnp.zeros((48, 128), BF16))
            parts.append(jnp.concatenate([up, block[48:96, :], down], axis=0))
        right = jnp.concatenate(parts, axis=1)
        feat = jnp.dot(weight[...], right, preferred_element_type=F32)
        both = jnp.concatenate([bias[...], bias[...]], axis=1)
        feat = (feat + both).astype(BF16)
        dec_ref[jnp.minimum(2 * m, slab_height - 1)] = feat[all_out:, 128:]
        dec_ref[jnp.abs(2 * m - 1)] = feat[all_out:, :128]
        value = feat[:all_out, :].astype(F32)
        halved = 0.5 * value
        buf[...] = (halved + halved * jnp.tanh(halved)).astype(BF16)

    def multiply(m, buf, slot):
        tap = jnp.dot(w1_ref[...], buf[...], preferred_element_type=F32)
        slot[0] = tap[:, :128]
        slot[1] = tap[:, 128:]

    def finish(m, before, slot):
        lines = (before.at[0], before.at[1], slot.at[0], slot.at[1])
        for n in range(2):
            y = 2 * m - 2 + n
            global_row = lax.rem(first_row + y, WPIX)
            sums = lines[n + 1][3 * outs : 6 * outs, :]
            sums = sums + jnp.where(global_row != 0, lines[n][0 : 3 * outs, :], 0.0)
            sums = sums + jnp.where(global_row != WPIX - 1, lines[n + 2][6 * outs :, :], 0.0)
            total = sums[outs : 2 * outs, :] + b1_ref[...]
            total = total + jnp.where(lane == 0, 0.0, pltpu.roll(sums[0:outs, :], 1, 1))
            total = total + jnp.where(lane == 127, 0.0, pltpu.roll(sums[2 * outs :, :], 127, 1))
            res_ref[y] = total.astype(BF16)

    acts = (act, act2)
    features(0, act)
    tap2[...] = jnp.zeros_like(tap2)
    tap3[...] = jnp.zeros_like(tap3)
    taps = (tap0, tap1, tap2, tap3)

    def several(step, carry):
        for n in range(12):
            m = 12 * step + 1 + n
            finish(jnp.maximum(m - 2, 1), taps[(n + 2) % 4], taps[(n + 3) % 4])
            features(m, acts[(n + 1) % 2])
            multiply(m - 1, acts[n % 2], taps[n % 4])
        return carry

    lax.fori_loop(0, rows // 12, several, 0)
    finish(rows - 1, taps[(rows - 2) % 4], taps[(rows - 1) % 4])
    multiply(rows, acts[rows % 2], taps[rows % 4])
    finish(rows, taps[(rows - 1) % 4], taps[rows % 4])


SPACES = {"s": pltpu.SMEM, "v": pltpu.VMEM, "h": pltpu.HBM}


def call(body, inputs, kinds, out_shape, scratch, flops, bytes_accessed, limit):
    return pl.pallas_call(
        body,
        out_shape=out_shape,
        in_specs=[pl.BlockSpec(memory_space=SPACES[k]) for k in kinds],
        out_specs=jax.tree.map(lambda _: pl.BlockSpec(memory_space=pltpu.VMEM), out_shape),
        scratch_shapes=scratch,
        compiler_params=pltpu.CompilerParams(vmem_limit_bytes=limit << 20),
        cost_estimate=pl.CostEstimate(flops=flops, bytes_accessed=bytes_accessed, transcendentals=0),
    )(*inputs)


def decode_call(rows, here, latents, weight, bias, w1, b1):
    width = latents.shape[1]
    outs = w1.shape[0] // 9
    channels = w1.shape[1]
    shape = jax.ShapeDtypeStruct((2 * rows, outs, WPIX), BF16)
    return call(
        functools.partial(decode_kernel, rows),
        (here, latents, weight, bias, w1, b1),
        "svvvvv",
        (shape, shape),
        [
            pltpu.VMEM((width, 512), F32),
            pltpu.VMEM((2 * (rows + 2) * 48, 128), BF16),
            pltpu.VMEM((channels, 256), BF16),
            pltpu.VMEM((channels, 256), BF16),
        ]
        + [pltpu.VMEM((2, 9 * outs, 128), F32)] * 4,
        6 * 10**9,
        3 * 10**6,
        24,
    )


def gather_call(here, recv, peers, outs):
    sds = jax.ShapeDtypeStruct
    many = (peers + 1) * outs
    return call(
        functools.partial(gather_kernel, peers),
        (here, recv),
        "sv",
        (sds((many, 144), BF16), sds((many, 128), F32)),
        [],
        10**6,
        10**6,
        8,
    )


def project_call(rows, peers, hidden, small):
    large = (hidden,) + small
    return call(
        functools.partial(project_kernel, rows, peers),
        large,
        "hhhhh",
        jax.ShapeDtypeStruct((peers * BLOCK, 128), BF16),
        [pltpu.VMEM(x.shape, x.dtype) for x in large]
        + [pltpu.VMEM((hidden.shape[1], 128), F32), pltpu.SemaphoreType.DMA((5,))],
        10**9,
        2 * 10**6,
        60,
    )


def clean_call(rows, peers, slabs, feats, recv, side):
    return call(
        functools.partial(clean_kernel, rows, peers, slabs, feats),
        (recv, side),
        "vv",
        jax.ShapeDtypeStruct((slabs * 8, 128), BF16),
        [],
        10**7,
        10**6,
        8,
    )


def pick_call(rows, peers, slabs, here, landed):
    width = 128 * (((rows + 2) // 2 + 1) // 2)
    return call(
        functools.partial(pick_kernel, rows, peers, slabs),
        (here, landed),
        "sv",
        jax.ShapeDtypeStruct((peers * 8, width), BF16),
        [pltpu.VMEM((slabs * 8, 128), F32)],
        10**6,
        10**6,
        8,
    )


def shards(
    hidden,
    modulation,
    final_weight,
    noisy,
    step_index,
    slab_table,
    conv_in_weight,
    conv_in_bias,
    conv1_weight,
    conv1_bias,
):
    peers = lax.axis_size("tensor")
    slabs = lax.axis_size("wide")
    t = lax.axis_index("tensor")
    w = lax.axis_index("wide")
    here = jnp.concatenate([jnp.stack([t, w]).astype(jnp.int32), step_index, slab_table])
    rows = slab_table.shape[0]
    feats = hidden.shape[1]
    outs = conv_in_weight.shape[1]
    sds = jax.ShapeDtypeStruct
    small = (modulation, final_weight.T, conv_in_weight.T, conv_in_bias.reshape(1, -1))
    send = project_call(rows, peers, hidden.T, small)
    side = call(
        functools.partial(side_kernel, rows, peers),
        (here, noisy.T),
        "sv",
        sds((2 * SR + 16, 128), F32),
        [pltpu.VMEM(noisy.shape, F32)],
        10**6,
        10**6,
        8,
    )
    recv = lax.all_to_all(send, "tensor", split_axis=0, concat_axis=0, tiled=True)
    routed = clean_call(rows, peers, slabs, feats, recv, side)
    landed = lax.all_to_all(routed, "wide", split_axis=0, concat_axis=0, tiled=True)
    copies = pick_call(rows, peers, slabs, here, landed)
    latents = lax.all_to_all(copies, "tensor", split_axis=0, concat_axis=0, tiled=True)
    own = lax.dynamic_slice_in_dim(conv1_weight, t * outs, outs, 2)
    w1 = own.transpose(0, 2, 1).reshape(9 * outs, -1)
    b1 = jnp.broadcast_to(lax.dynamic_slice_in_dim(conv1_bias, t * outs, outs, 0)[:, None], (outs, 128))
    weight, bias = gather_call(here, recv, peers, outs)
    return decode_call(rows, here, latents, weight, bias, w1, b1)


def solution(mesh):
    return jax.shard_map(
        shards,
        mesh=mesh,
        in_specs=(
            P("wide", "tensor"),
            P(None, "tensor"),
            P("tensor", None),
            P("wide", None),
            P(),
            P("wide"),
            P(None, "tensor"),
            P("tensor"),
            P(),
            P(),
        ),
        out_specs=(P("wide", "tensor", None), P("wide", "tensor", None)),
        check_vma=False,
    )
```

```python
import functools

import jax
import jax.numpy as jnp
from jax import lax
from jax.experimental import pallas as pl
from jax.experimental.pallas import tpu as pltpu
from jax.sharding import PartitionSpec as P

D = 3072
LC = 16
GRID = 64
STEPS = 28
WPIX = 128
shift_value = 3.0
norm_eps = 1e-06

F32 = jnp.float32
BF16 = jnp.bfloat16

SR = 24
STAT = 2 * SR
WROW = STAT + 16
BLOCK = WROW + 32


def iota(shape, dim):
    return lax.broadcasted_iota(jnp.int32, shape, dim)


def thirds(value):
    first = value.astype(BF16).astype(F32)
    rest = value - first
    second = rest.astype(BF16).astype(F32)
    return (first, second, (rest - second).astype(BF16).astype(F32))


def to_column(row):
    n = row.shape[1]
    return jnp.sum(jnp.where(iota((n, n), 0) == iota((n, n), 1), row, 0.0), axis=1, keepdims=True)


def to_row(column):
    n = column.shape[0]
    return jnp.sum(jnp.where(iota((n, n), 0) == iota((n, n), 1), column, 0.0), axis=0, keepdims=True)


def project_kernel(rows, peers, h_hbm, *rest):
    small = rest[:4]
    send_ref, h_ref, mod_ref, w_ref, win_ref, bin_ref, sums, sems = rest[4:]
    moves = list(zip(small, (mod_ref, w_ref, win_ref, bin_ref)))
    moves.append((h_hbm, h_ref))
    copies = [pltpu.make_async_copy(src, dst, sems.at[n]) for n, (src, dst) in enumerate(moves)]
    for copy in copies:
        copy.start()
    for copy in copies[:4]:
        copy.wait()
    per = GRID // peers
    feats = h_ref.shape[0]
    weight = w_ref[...].astype(F32)
    scaled = (1.0 + mod_ref[1:2, :]) * weight
    colsum = jnp.sum(scaled, axis=1, keepdims=True)
    shifted = jnp.sum(mod_ref[0:1, :] * weight, axis=1, keepdims=True)
    left = jnp.concatenate(thirds(scaled - colsum / feats), axis=0).astype(BF16)
    lane = iota((1, 128), 1)
    low = lane < 64
    step = 256
    copies[4].wait()
    for at in range(0, h_ref.shape[1], step):
        hid = h_ref[:, at : at + step]
        prod = jnp.dot(left, hid, preferred_element_type=F32)
        wide = hid.astype(F32)
        pieces = thirds(jnp.sum(wide, axis=0, keepdims=True)) + thirds(jnp.sum(wide * wide, axis=0, keepdims=True))
        stats = [jnp.broadcast_to(p, (4, step)) for p in pieces] + [jnp.zeros((40, step), F32)]
        both = jnp.concatenate([prod[:64, :] + prod[64:128, :] + prod[128:, :]] + stats, axis=0)
        sums[at : at + step, :] = jnp.transpose(both)
    win = win_ref[...].astype(F32)
    outs = win.shape[0]
    rest_w = jnp.concatenate([win[:, 128:], jnp.zeros((outs, 128 - (win.shape[1] - 128)), F32)], axis=1)
    bias = jnp.zeros((outs, 128), F32)
    for n, piece in enumerate(thirds(to_column(bin_ref[...]))):
        bias = jnp.where(lane == n, piece, bias)
    pad = jnp.zeros((1, 64), F32)
    lines = thirds(to_row(colsum)) + thirds(to_row(shifted))
    lower = jnp.concatenate([jnp.concatenate([v, pad], axis=1) for v in lines] + [jnp.zeros((2, 128), F32)], axis=0)
    upper = jnp.zeros((8, 128), F32)
    for g in range(outs // 8):
        upper = upper + pltpu.roll(bias[8 * g : 8 * g + 8, :], 72 + 4 * g, 1)
        lower = lower + pltpu.roll(rest_w[8 * g : 8 * g + 8, :], 64 + 16 * g, 1)
    main_w = win_ref[:, :128]
    fill = [jnp.zeros((SR - rows, 128), F32)] if rows < SR else []
    for peer in range(peers):
        base = peer * BLOCK
        stat = jnp.zeros((SR, 128), F32)
        halves = []
        for dk in range(per):
            val = sums[pl.ds(peer * per + dk, rows, stride=GRID), :]
            val = jnp.concatenate([val] + fill, axis=0) if fill else val
            turned = pltpu.roll(val, 64, 1)
            stat = jnp.where((lane % 4 == dk) & (lane < 24), turned, stat)
            halves.append(val if dk % 2 == 0 else turned)
        for half in range(per // 2):
            joined = jnp.where(low, halves[2 * half], halves[2 * half + 1])
            send_ref[base + half * SR : base + (half + 1) * SR, :] = joined.astype(BF16)
        tile = upper
        for g in range(SR // 8):
            tile = tile + (pltpu.roll(stat[8 * g : 8 * g + 8, :], 24 * g, 1) if g else stat[:8, :])
        send_ref[base + STAT : base + STAT + 16, :] = jnp.concatenate([tile, lower], axis=0).astype(BF16)
        send_ref[base + WROW : base + WROW + 32, :] = main_w


def side_kernel(rows, peers, slabs, here, noisy_ref, side_ref, route_ref, choose_ref, drawn):
    per = GRID // peers
    lane = iota((1, 128), 1)
    fill = [jnp.zeros((SR - rows, 128), F32)] if rows < SR else []
    owner = jnp.full((1, 128), -9, jnp.int32)
    for j in range(rows):
        owner = jnp.where((lane % SR == j) & (lane < 4 * SR), here[3 + j], owner)
    shape = (slabs * 8, 128)
    row = iota(shape, 0)
    col = iota(shape, 1)
    slab = row // 8
    upper = row % 8 < 4
    dk = row % 4
    turned = col // (2 * SR)
    half = (col // SR) % 2
    j = col % SR
    right_half = half == dk // 2
    target = jnp.where(upper, owner, jnp.where(j == 0, owner - 1, -9))
    own = target == slab
    take_low = (right_half & (turned == dk % 2) & own).astype(F32).astype(BF16)
    above = upper & (j == rows - 1) & (owner + 1 == slab) & (owner >= 0)
    take_high = (right_half & (turned == 1 - dk % 2) & above).astype(F32).astype(BF16)
    route_ref[: slabs * 8, :] = take_low
    route_ref[slabs * 8 :, :] = take_high
    frac = (jnp.zeros((8, 128), F32) + here[2].astype(F32)) / STEPS
    sigma = shift_value * frac / (1.0 + (shift_value - 1.0) * frac)
    side_ref[2 * SR :, :] = sigma
    for at in range(0, noisy_ref.shape[1], 256):
        drawn[at : at + 256, :] = jnp.transpose(noisy_ref[:, at : at + 256])
    mine = here[0] * per
    for half in range(per // 2):
        one = drawn[pl.ds(mine + 2 * half, rows, stride=GRID), :]
        two = drawn[pl.ds(mine + 2 * half + 1, rows, stride=GRID), :]
        both = jnp.concatenate([one, two], axis=1)
        side_ref[half * SR : (half + 1) * SR, :] = jnp.concatenate([both] + fill, axis=0) if fill else both

    count = rows + 2
    half_rows = count // 2
    blocks = (half_rows + 1) // 2
    row = iota((blocks * 8, 128), 0)
    picked = [jnp.full((blocks * 8, 128), -1, jnp.int32) for _ in range(4)]

    def source(j):
        return lax.rem(2 * here[1] - here[3 + j] + 2 * slabs, slabs)

    for i in range(count):
        n = i % half_rows
        if i == 0:
            at, is_low = (lax.rem(source(rows - 1) - 1 + slabs, slabs) * 8, False)
        elif i == count - 1:
            at, is_low = (lax.rem(source(0) + 1, slabs) * 8 + 4, True)
        else:
            at, is_low = (source(i - 1) * 8, True)
        group = (0 if is_low else 1) if n % 2 == 0 else (2 if is_low else 3)
        mine = row // 4 == 2 * (n // 2) + i // half_rows
        picked[group] = jnp.where(mine, at + row % 4, picked[group])
    wanted = jnp.concatenate(picked, axis=0)
    column = iota((1, 128), 1)
    for at in range(0, slabs * 8, 128):
        choose_ref[:, at : at + 128] = (wanted == column + at).astype(F32).astype(BF16)


def spread(tile, at, low):
    parts = []
    for half in range(2):
        a = tile[:, at + 2 * half : at + 2 * half + 1]
        b = tile[:, at + 2 * half + 1 : at + 2 * half + 2]
        parts.append(jnp.where(low, a, b))
    return jnp.concatenate(parts, axis=0)


def clean_kernel(peers, feats, recv_ref, side_ref, route_ref, send_ref):
    lane = iota((1, 128), 1)
    low = lane < 64
    total = jnp.zeros((2 * SR, 128), F32)
    means = []
    columns = []
    sums = jnp.zeros((SR, 128), F32)
    shifted = jnp.zeros((1, 128), F32)
    for peer in range(peers):
        base = peer * BLOCK
        total = total + recv_ref[base : base + 2 * SR, :].astype(F32)
        tile = recv_ref[base + STAT : base + STAT + 16, :].astype(F32)
        upper = tile[:8, :]
        lines = tile[8:, :]
        stat = jnp.concatenate([upper, pltpu.roll(upper, 104, 1), pltpu.roll(upper, 80, 1)], axis=0)
        stat = stat + pltpu.roll(stat, 124, 1) + pltpu.roll(stat, 120, 1)
        sums = sums + stat
        means.append(stat / feats)
        cs = jnp.where(low, lines[0:1, :] + lines[1:2, :] + lines[2:3, :], 0.0)
        columns.append(cs + pltpu.roll(cs, 64, 1))
        sw = jnp.where(low, lines[3:4, :] + lines[4:5, :] + lines[5:6, :], 0.0)
        shifted = shifted + sw + pltpu.roll(sw, 64, 1)
    mean = sums / (feats * peers)
    for m, cs in zip(means, columns):
        total = total + spread(m - mean, 0, low) * cs
    square = pltpu.roll(mean, 116, 1)
    rstd = 1.0 / jnp.sqrt(square - mean * mean + norm_eps)
    velocity = total * spread(rstd, 0, low) + shifted
    sigma = side_ref[2 * SR : 2 * SR + 1, :]
    clean = (side_ref[: 2 * SR, :] - sigma * velocity).astype(BF16).astype(F32)
    held = jnp.concatenate([clean, pltpu.roll(clean, 64, 1), jnp.zeros((128 - 4 * SR, 128), F32)], axis=0).astype(BF16)
    both = jnp.dot(route_ref[...], held, preferred_element_type=F32)
    count = both.shape[0] // 2
    send_ref[...] = jnp.where(low, both[:count, :], both[count:, :]).astype(BF16)


def pick_kernel(peers, choose_ref, recv_ref, send_ref):
    low = iota((1, 128), 1) < 64
    rows = jnp.dot(choose_ref[...], recv_ref[...], preferred_element_type=F32)
    group = rows.shape[0] // 4
    left = rows[:group, :] + pltpu.roll(rows[group : 2 * group, :], 64, 1)
    right = pltpu.roll(rows[2 * group : 3 * group, :], 64, 1) + rows[3 * group :, :]
    tiles = jnp.where(low, left, right).astype(BF16)
    for block in range(group // 8):
        tile = tiles[block * 8 : block * 8 + 8, :]
        for peer in range(peers):
            send_ref[peer * 8 : peer * 8 + 8, block * 128 : (block + 1) * 128] = tile


def gather_kernel(peers, here, recv_ref, weight, bias):
    lane = iota((1, 128), 1)
    outs = weight.shape[0] // (peers + 1)

    def load(base, at):
        tile = recv_ref[pl.ds(pl.multiple_of(base + STAT, 16), 16), :].astype(F32)
        groups = range(outs // 8)
        side = jnp.concatenate([pltpu.roll(tile[8:, :], 64 - 16 * g, 1) for g in groups], axis=0)
        turned = jnp.concatenate([pltpu.roll(tile[:8, :], 56 - 4 * g, 1) for g in groups], axis=0)
        weight[at : at + outs, :128] = recv_ref[pl.ds(pl.multiple_of(base + WROW, 16), 32), :]
        weight[at : at + outs, 128:] = side[:, :16].astype(BF16)
        total = turned[:, 0:1] + turned[:, 1:2] + turned[:, 2:3]
        bias[at : at + outs, :] = jnp.broadcast_to(total, (outs, 128))

    for peer in range(peers):
        load(peer * BLOCK, peer * outs)
    load(here[0] * BLOCK, peers * outs)


def decode_kernel(rows, here, lat_ref, weight, bias, w1_ref, b1_ref, dec_ref, res_ref, spread_out, shifted, act, act2, tap0, tap1, tap2, tap3):
    slab_height = 2 * rows
    first_row = here[1] * slab_height
    count = rows + 2
    per = count // 2
    outs = w1_ref.shape[0] // 9
    lane = iota((1, 128), 1)
    all_out = w1_ref.shape[1]

    r = iota((128, 512), 0)
    c = iota((128, 512), 1)
    token = 4 * (r // 8) + r % 4
    hot = ((r // 4) % 2 == c // 256) & (c % 128 == 2 * token + (c // 128) % 2)
    hot = hot.astype(F32).astype(BF16)
    spread_out[...] = lax.dot_general(lat_ref[...], hot, (((0,), (0,)), ((), ())), preferred_element_type=F32)
    for i in range(count):
        for a in range(2):
            at = (i % per) * 64 + a * 32
            base = (i // per) * 256
            pix = spread_out[at : at + 16, base : base + 128] + spread_out[at + 16 : at + 32, base + 128 : base + 256]
            row = (2 * i + a) * 48
            shifted[row : row + 16, :] = jnp.where(lane == 0, 0.0, pltpu.roll(pix, 1, 1)).astype(BF16)
            shifted[row + 16 : row + 32, :] = pix.astype(BF16)
            shifted[row + 32 : row + 48, :] = jnp.where(lane == 127, 0.0, pltpu.roll(pix, 127, 1)).astype(BF16)

    def features(m, buf):
        parts = []
        for n in range(2):
            q = 2 * m + n
            global_row = lax.rem(first_row - 1 + q + WPIX, WPIX)
            block = shifted[q * 48 : q * 48 + 144, :]
            up = jnp.where(global_row != 0, block[:48, :], jnp.zeros((48, 128), BF16))
            down = jnp.where(global_row != WPIX - 1, block[96:, :], jnp.zeros((48, 128), BF16))
            parts.append(jnp.concatenate([up, block[48:96, :], down], axis=0))
        right = jnp.concatenate(parts, axis=1)
        feat = jnp.dot(weight[...], right, preferred_element_type=F32)
        both = jnp.concatenate([bias[...], bias[...]], axis=1)
        feat = (feat + both).astype(BF16)
        if m > 0:
            dec_ref[2 * m - 1] = feat[all_out:, :128]
        if m < rows:
            dec_ref[2 * m] = feat[all_out:, 128:]
        value = feat[:all_out, :].astype(F32)
        halved = 0.5 * value
        buf[...] = (halved + halved * jnp.tanh(halved)).astype(BF16)

    def multiply(m, buf, slot):
        tap = jnp.dot(w1_ref[...], buf[...], preferred_element_type=F32)
        slot[0] = tap[:, :128]
        slot[1] = tap[:, 128:]

    def finish(m, before, slot):
        lines = (before.at[0], before.at[1], slot.at[0], slot.at[1])
        for n in range(2):
            y = 2 * m - 2 + n
            global_row = lax.rem(first_row + y, WPIX)
            sums = lines[n + 1][3 * outs : 6 * outs, :]
            sums = sums + jnp.where(global_row != 0, lines[n][0 : 3 * outs, :], 0.0)
            sums = sums + jnp.where(global_row != WPIX - 1, lines[n + 2][6 * outs :, :], 0.0)
            total = sums[outs : 2 * outs, :] + b1_ref[...]
            total = total + jnp.where(lane == 0, 0.0, pltpu.roll(sums[0:outs, :], 1, 1))
            total = total + jnp.where(lane == 127, 0.0, pltpu.roll(sums[2 * outs :, :], 127, 1))
            res_ref[y] = total.astype(BF16)

    acts = (act, act2)
    taps = (tap0, tap1, tap2, tap3)
    features(0, act)
    for m in range(1, rows + 1):
        if m > 2:
            finish(m - 2, taps[(m + 1) % 4], taps[(m + 2) % 4])
        features(m, acts[m % 2])
        multiply(m - 1, acts[(m - 1) % 2], taps[(m - 1) % 4])
    finish(rows - 1, taps[(rows - 2) % 4], taps[(rows - 1) % 4])
    multiply(rows, acts[rows % 2], taps[rows % 4])
    finish(rows, taps[(rows - 1) % 4], taps[rows % 4])


SPACES = {"s": pltpu.SMEM, "v": pltpu.VMEM, "h": pltpu.HBM}


def call(body, inputs, kinds, out_shape, scratch, flops, bytes_accessed, limit):
    return pl.pallas_call(
        body,
        out_shape=out_shape,
        in_specs=[pl.BlockSpec(memory_space=SPACES[k]) for k in kinds],
        out_specs=jax.tree.map(lambda _: pl.BlockSpec(memory_space=pltpu.VMEM), out_shape),
        scratch_shapes=scratch,
        compiler_params=pltpu.CompilerParams(vmem_limit_bytes=limit << 20),
        cost_estimate=pl.CostEstimate(flops=flops, bytes_accessed=bytes_accessed, transcendentals=0),
    )(*inputs)


def decode_call(rows, here, latents, weight, bias, w1, b1):
    width = latents.shape[1]
    outs = w1.shape[0] // 9
    channels = w1.shape[1]
    shape = jax.ShapeDtypeStruct((2 * rows, outs, WPIX), BF16)
    return call(
        functools.partial(decode_kernel, rows),
        (here, latents, weight, bias, w1, b1),
        "svvvvv",
        (shape, shape),
        [
            pltpu.VMEM((width, 512), F32),
            pltpu.VMEM((2 * (rows + 2) * 48, 128), BF16),
            pltpu.VMEM((channels, 256), BF16),
            pltpu.VMEM((channels, 256), BF16),
        ]
        + [pltpu.VMEM((2, 9 * outs, 128), F32)] * 4,
        6 * 10**9,
        3 * 10**6,
        24,
    )


def gather_call(here, recv, peers, outs):
    sds = jax.ShapeDtypeStruct
    many = (peers + 1) * outs
    return call(
        functools.partial(gather_kernel, peers),
        (here, recv),
        "sv",
        (sds((many, 144), BF16), sds((many, 128), F32)),
        [],
        10**6,
        10**6,
        8,
    )


def project_call(rows, peers, hidden, small):
    large = (hidden,) + small
    return call(
        functools.partial(project_kernel, rows, peers),
        large,
        "hhhhh",
        jax.ShapeDtypeStruct((peers * BLOCK, 128), BF16),
        [pltpu.VMEM(x.shape, x.dtype) for x in large]
        + [pltpu.VMEM((hidden.shape[1], 128), F32), pltpu.SemaphoreType.DMA((5,))],
        10**9,
        2 * 10**6,
        60,
    )


def clean_call(peers, slabs, feats, recv, side, route):
    return call(
        functools.partial(clean_kernel, peers, feats),
        (recv, side, route),
        "vvv",
        jax.ShapeDtypeStruct((slabs * 8, 128), BF16),
        [],
        10**7,
        10**6,
        8,
    )


def pick_call(peers, choose, landed):
    return call(
        functools.partial(pick_kernel, peers),
        (choose, landed),
        "vv",
        jax.ShapeDtypeStruct((peers * 8, choose.shape[0] // 32 * 128), BF16),
        [],
        10**7,
        10**6,
        8,
    )


def shards(
    hidden,
    modulation,
    final_weight,
    noisy,
    step_index,
    slab_table,
    conv_in_weight,
    conv_in_bias,
    conv1_weight,
    conv1_bias,
):
    peers = lax.axis_size("tensor")
    slabs = lax.axis_size("wide")
    t = lax.axis_index("tensor")
    w = lax.axis_index("wide")
    here = jnp.concatenate([jnp.stack([t, w]).astype(jnp.int32), step_index, slab_table])
    rows = slab_table.shape[0]
    feats = hidden.shape[1]
    outs = conv_in_weight.shape[1]
    sds = jax.ShapeDtypeStruct
    small = (modulation, final_weight.T, conv_in_weight.T, conv_in_bias.reshape(1, -1))
    send = project_call(rows, peers, hidden.T, small)
    blocks = ((rows + 2) // 2 + 1) // 2
    side, route, choose = call(
        functools.partial(side_kernel, rows, peers, slabs),
        (here, noisy.T),
        "sv",
        (sds((2 * SR + 8, 128), F32), sds((2 * slabs * 8, 128), BF16), sds((4 * blocks * 8, slabs * 8), BF16)),
        [pltpu.VMEM(noisy.shape, F32)],
        10**6,
        10**6,
        8,
    )
    recv = lax.all_to_all(send, "tensor", split_axis=0, concat_axis=0, tiled=True)
    routed = clean_call(peers, slabs, feats, recv, side, route)
    landed = lax.all_to_all(routed, "wide", split_axis=0, concat_axis=0, tiled=True)
    copies = pick_call(peers, choose, landed)
    latents = lax.all_to_all(copies, "tensor", split_axis=0, concat_axis=0, tiled=True)
    own = lax.dynamic_slice_in_dim(conv1_weight, t * outs, outs, 2)
    w1 = own.transpose(0, 2, 1).reshape(9 * outs, -1)
    b1 = jnp.broadcast_to(lax.dynamic_slice_in_dim(conv1_bias, t * outs, outs, 0)[:, None], (outs, 128))
    weight, bias = gather_call(here, recv, peers, outs)
    return decode_call(rows, here, latents, weight, bias, w1, b1)


def solution(mesh):
    return jax.shard_map(
        shards,
        mesh=mesh,
        in_specs=(
            P("wide", "tensor"),
            P(None, "tensor"),
            P("tensor", None),
            P("wide", None),
            P(),
            P("wide"),
            P(None, "tensor"),
            P("tensor"),
            P(),
            P(),
        ),
        out_specs=(P("wide", "tensor", None), P("wide", "tensor", None)),
        check_vma=False,
    )
```

```python
import functools

import jax
import jax.numpy as jnp
from jax import lax
from jax.experimental import pallas as pl
from jax.experimental.pallas import tpu as pltpu
from jax.sharding import PartitionSpec as P

D = 3072
LC = 16
GRID = 64
STEPS = 28
WPIX = 128
shift_value = 3.0
norm_eps = 1e-06

F32 = jnp.float32
BF16 = jnp.bfloat16

SR = 24
STAT = 2 * SR
BLOCK = STAT + 16
WBLOCK = 48
STEPS_AWAY = (8, 4, 2, 1)


def iota(shape, dim):
    return lax.broadcasted_iota(jnp.int32, shape, dim)


def thirds(value):
    first = value.astype(BF16).astype(F32)
    rest = value - first
    second = rest.astype(BF16).astype(F32)
    return (first, second, (rest - second).astype(BF16).astype(F32))


def to_column(row):
    n = row.shape[1]
    return jnp.sum(jnp.where(iota((n, n), 0) == iota((n, n), 1), row, 0.0), axis=1, keepdims=True)


def to_row(column):
    n = column.shape[0]
    return jnp.sum(jnp.where(iota((n, n), 0) == iota((n, n), 1), column, 0.0), axis=0, keepdims=True)


def project_kernel(rows, peers, h_hbm, *rest):
    small = rest[:4]
    send_ref, weight_ref, h_ref, mod_ref, w_ref, win_ref, bin_ref, sums, sems = rest[4:]
    moves = list(zip(small, (mod_ref, w_ref, win_ref, bin_ref)))
    moves.append((h_hbm, h_ref))
    copies = [pltpu.make_async_copy(src, dst, sems.at[n]) for n, (src, dst) in enumerate(moves)]
    for copy in copies:
        copy.start()
    for copy in copies[:4]:
        copy.wait()
    per = GRID // peers
    feats = h_ref.shape[0]
    weight = w_ref[...].astype(F32)
    scaled = (1.0 + mod_ref[1:2, :]) * weight
    colsum = jnp.sum(scaled, axis=1, keepdims=True)
    shifted = jnp.sum(mod_ref[0:1, :] * weight, axis=1, keepdims=True)
    left = jnp.concatenate(thirds(scaled - colsum / feats), axis=0).astype(BF16)
    lane = iota((1, 128), 1)
    low = lane < 64
    step = 256
    copies[4].wait()
    for at in range(0, h_ref.shape[1], step):
        hid = h_ref[:, at : at + step]
        prod = jnp.dot(left, hid, preferred_element_type=F32)
        wide = hid.astype(F32)
        pieces = thirds(jnp.sum(wide, axis=0, keepdims=True)) + thirds(jnp.sum(wide * wide, axis=0, keepdims=True))
        stats = [jnp.broadcast_to(p, (4, step)) for p in pieces] + [jnp.zeros((40, step), F32)]
        both = jnp.concatenate([prod[:64, :] + prod[64:128, :] + prod[128:, :]] + stats, axis=0)
        sums[at : at + step, :] = jnp.transpose(both)
    win = win_ref[...].astype(F32)
    outs = win.shape[0]
    rest_w = jnp.concatenate([win[:, 128:], jnp.zeros((outs, 128 - (win.shape[1] - 128)), F32)], axis=1)
    bias = jnp.zeros((outs, 128), F32)
    for n, piece in enumerate(thirds(to_column(bin_ref[...]))):
        bias = jnp.where(lane == n, piece, bias)
    pad = jnp.zeros((1, 64), F32)
    lines = thirds(to_row(colsum)) + thirds(to_row(shifted))
    lower = jnp.concatenate([jnp.concatenate([v, pad], axis=1) for v in lines] + [jnp.zeros((2, 128), F32)], axis=0)
    ends = jnp.zeros((8, 128), F32)
    for g in range(outs // 8):
        ends = ends + pltpu.roll(bias[8 * g : 8 * g + 8, :], 64 + 4 * g, 1)
        ends = ends + (pltpu.roll(rest_w[8 * g : 8 * g + 8, :], 16 * g, 1) if g else rest_w[:8, :])
    held = jnp.concatenate([win[:, :128], ends, jnp.zeros((WBLOCK - outs - 8, 128), F32)], axis=0).astype(BF16)
    weight_ref[...] = held
    fill = [jnp.zeros((SR - rows, 128), F32)] if rows < SR else []
    for peer in range(peers):
        base = peer * BLOCK
        stat = jnp.zeros((SR, 128), F32)
        halves = []
        for dk in range(per):
            val = sums[pl.ds(peer * per + dk, rows, stride=GRID), :]
            val = jnp.concatenate([val] + fill, axis=0) if fill else val
            turned = pltpu.roll(val, 64, 1)
            stat = jnp.where((lane % 4 == dk) & (lane < 24), turned, stat)
            halves.append(val if dk % 2 == 0 else turned)
        for half in range(per // 2):
            joined = jnp.where(low, halves[2 * half], halves[2 * half + 1])
            send_ref[base + half * SR : base + (half + 1) * SR, :] = joined.astype(BF16)
        tile = stat[:8, :]
        for g in range(1, SR // 8):
            tile = tile + pltpu.roll(stat[8 * g : 8 * g + 8, :], 24 * g, 1)
        send_ref[base + STAT : base + STAT + 16, :] = jnp.concatenate([tile, lower], axis=0).astype(BF16)


def side_kernel(rows, peers, slabs, here, noisy_ref, side_ref, route_ref, choose_ref, drawn):
    per = GRID // peers
    lane = iota((1, 128), 1)
    fill = [jnp.zeros((SR - rows, 128), F32)] if rows < SR else []
    owner = jnp.full((1, 128), -9, jnp.int32)
    for j in range(rows):
        owner = jnp.where((lane % SR == j) & (lane < 4 * SR), here[3 + j], owner)
    shape = (slabs * 8, 128)
    row = iota(shape, 0)
    col = iota(shape, 1)
    slab = row // 8
    upper = row % 8 < 4
    dk = row % 4
    turned = col // (2 * SR)
    half = (col // SR) % 2
    j = col % SR
    right_half = half == dk // 2
    target = jnp.where(upper, owner, jnp.where(j == 0, owner - 1, -9))
    own = target == slab
    take_low = (right_half & (turned == dk % 2) & own).astype(F32).astype(BF16)
    above = upper & (j == rows - 1) & (owner + 1 == slab) & (owner >= 0)
    take_high = (right_half & (turned == 1 - dk % 2) & above).astype(F32).astype(BF16)
    route_ref[: slabs * 8, :] = take_low
    route_ref[slabs * 8 :, :] = take_high
    frac = (jnp.zeros((8, 128), F32) + here[2].astype(F32)) / STEPS
    sigma = shift_value * frac / (1.0 + (shift_value - 1.0) * frac)
    side_ref[2 * SR :, :] = sigma
    for at in range(0, noisy_ref.shape[1], 256):
        drawn[at : at + 256, :] = jnp.transpose(noisy_ref[:, at : at + 256])
    mine = here[0] * per
    for half in range(per // 2):
        one = drawn[pl.ds(mine + 2 * half, rows, stride=GRID), :]
        two = drawn[pl.ds(mine + 2 * half + 1, rows, stride=GRID), :]
        both = jnp.concatenate([one, two], axis=1)
        side_ref[half * SR : (half + 1) * SR, :] = jnp.concatenate([both] + fill, axis=0) if fill else both

    count = rows + 2
    half_rows = count // 2
    blocks = (half_rows + 1) // 2
    row = iota((blocks * 8, 128), 0)
    picked = [jnp.full((blocks * 8, 128), -1, jnp.int32) for _ in range(4)]

    def source(j):
        return lax.rem(2 * here[1] - here[3 + j] + 2 * slabs, slabs)

    for i in range(count):
        n = i % half_rows
        if i == 0:
            at, is_low = (lax.rem(source(rows - 1) - 1 + slabs, slabs) * 8, False)
        elif i == count - 1:
            at, is_low = (lax.rem(source(0) + 1, slabs) * 8 + 4, True)
        else:
            at, is_low = (source(i - 1) * 8, True)
        group = (0 if is_low else 1) if n % 2 == 0 else (2 if is_low else 3)
        mine = row // 4 == 2 * (n // 2) + i // half_rows
        picked[group] = jnp.where(mine, at + row % 4, picked[group])
    wanted = jnp.concatenate(picked, axis=0)
    column = iota((1, 128), 1)
    for at in range(0, slabs * 8, 128):
        choose_ref[:, at : at + 128] = (wanted == column + at).astype(F32).astype(BF16)


def spread(tile, at, low):
    parts = []
    for half in range(2):
        a = tile[:, at + 2 * half : at + 2 * half + 1]
        b = tile[:, at + 2 * half + 1 : at + 2 * half + 2]
        parts.append(jnp.where(low, a, b))
    return jnp.concatenate(parts, axis=0)


def clean_kernel(peers, feats, recv_ref, side_ref, route_ref, send_ref):
    lane = iota((1, 128), 1)
    low = lane < 64
    total = jnp.zeros((2 * SR, 128), F32)
    means = []
    columns = []
    sums = jnp.zeros((SR, 128), F32)
    shifted = jnp.zeros((1, 128), F32)
    for peer in range(peers):
        base = peer * BLOCK
        total = total + recv_ref[base : base + 2 * SR, :].astype(F32)
        tile = recv_ref[base + STAT : base + STAT + 16, :].astype(F32)
        upper = tile[:8, :]
        lines = tile[8:, :]
        stat = jnp.concatenate([upper, pltpu.roll(upper, 104, 1), pltpu.roll(upper, 80, 1)], axis=0)
        stat = stat + pltpu.roll(stat, 124, 1) + pltpu.roll(stat, 120, 1)
        sums = sums + stat
        means.append(stat / feats)
        cs = jnp.where(low, lines[0:1, :] + lines[1:2, :] + lines[2:3, :], 0.0)
        columns.append(cs + pltpu.roll(cs, 64, 1))
        sw = jnp.where(low, lines[3:4, :] + lines[4:5, :] + lines[5:6, :], 0.0)
        shifted = shifted + sw + pltpu.roll(sw, 64, 1)
    mean = sums / (feats * peers)
    for m, cs in zip(means, columns):
        total = total + spread(m - mean, 0, low) * cs
    square = pltpu.roll(mean, 116, 1)
    rstd = 1.0 / jnp.sqrt(square - mean * mean + norm_eps)
    velocity = total * spread(rstd, 0, low) + shifted
    sigma = side_ref[2 * SR : 2 * SR + 1, :]
    clean = (side_ref[: 2 * SR, :] - sigma * velocity).astype(BF16).astype(F32)
    held = jnp.concatenate([clean, pltpu.roll(clean, 64, 1), jnp.zeros((128 - 4 * SR, 128), F32)], axis=0).astype(BF16)
    both = jnp.dot(route_ref[...], held, preferred_element_type=F32)
    count = both.shape[0] // 2
    send_ref[...] = jnp.where(low, both[:count, :], both[count:, :]).astype(BF16)


def pick_kernel(peers, choose_ref, recv_ref, send_ref):
    low = iota((1, 128), 1) < 64
    rows = jnp.dot(choose_ref[...], recv_ref[...], preferred_element_type=F32)
    group = rows.shape[0] // 4
    left = rows[:group, :] + pltpu.roll(rows[group : 2 * group, :], 64, 1)
    right = pltpu.roll(rows[2 * group : 3 * group, :], 64, 1) + rows[3 * group :, :]
    tiles = jnp.where(low, left, right).astype(BF16)
    for block in range(group // 8):
        tile = tiles[block * 8 : block * 8 + 8, :]
        for peer in range(peers):
            send_ref[peer * 8 : peer * 8 + 8, block * 128 : (block + 1) * 128] = tile


def gather_kernel(peers, here, recv_ref, weight, bias):
    lane = iota((1, 128), 1)
    outs = weight.shape[0] // (peers + 1)

    def load(base, at):
        block = recv_ref[base : base + WBLOCK, :]
        tile = block[outs : outs + 8, :].astype(F32)
        groups = range(outs // 8)
        side = jnp.concatenate([pltpu.roll(tile, 128 - 16 * g, 1) if g else tile for g in groups], axis=0)
        turned = jnp.concatenate([pltpu.roll(tile, 64 - 4 * g, 1) for g in groups], axis=0)
        at = pl.ds(pl.multiple_of(at * outs, outs), outs)
        weight[at, :128] = block[:outs, :]
        weight[at, 128:] = side[:, :16].astype(BF16)
        total = turned[:, 0:1] + turned[:, 1:2] + turned[:, 2:3]
        bias[at, :] = jnp.broadcast_to(total, (outs, 128))

    for slot in range(peers):
        away = sum(bit for n, bit in enumerate(STEPS_AWAY) if slot >> n & 1)
        load(slot * WBLOCK, jnp.bitwise_xor(here[0], away))
    load(0, peers)


def decode_kernel(rows, here, lat_ref, weight, bias, w1_ref, b1_ref, dec_ref, res_ref, spread_out, shifted, act, act2, tap0, tap1, tap2, tap3):
    slab_height = 2 * rows
    first_row = here[1] * slab_height
    count = rows + 2
    per = count // 2
    outs = w1_ref.shape[0] // 9
    lane = iota((1, 128), 1)
    all_out = w1_ref.shape[1]

    r = iota((128, 512), 0)
    c = iota((128, 512), 1)
    token = 4 * (r // 8) + r % 4
    hot = ((r // 4) % 2 == c // 256) & (c % 128 == 2 * token + (c // 128) % 2)
    hot = hot.astype(F32).astype(BF16)
    spread_out[...] = lax.dot_general(lat_ref[...], hot, (((0,), (0,)), ((), ())), preferred_element_type=F32)
    for i in range(count):
        for a in range(2):
            at = (i % per) * 64 + a * 32
            base = (i // per) * 256
            pix = spread_out[at : at + 16, base : base + 128] + spread_out[at + 16 : at + 32, base + 128 : base + 256]
            row = (2 * i + a) * 48
            shifted[row : row + 16, :] = jnp.where(lane == 0, 0.0, pltpu.roll(pix, 1, 1)).astype(BF16)
            shifted[row + 16 : row + 32, :] = pix.astype(BF16)
            shifted[row + 32 : row + 48, :] = jnp.where(lane == 127, 0.0, pltpu.roll(pix, 127, 1)).astype(BF16)

    def features(m, buf):
        parts = []
        for n in range(2):
            q = 2 * m + n
            global_row = lax.rem(first_row - 1 + q + WPIX, WPIX)
            block = shifted[pl.ds(pl.multiple_of(q * 48, 16), 144), :]
            up = jnp.where(global_row != 0, block[:48, :], jnp.zeros((48, 128), BF16))
            down = jnp.where(global_row != WPIX - 1, block[96:, :], jnp.zeros((48, 128), BF16))
            parts.append(jnp.concatenate([up, block[48:96, :], down], axis=0))
        right = jnp.concatenate(parts, axis=1)
        feat = jnp.dot(weight[...], right, preferred_element_type=F32)
        both = jnp.concatenate([bias[...], bias[...]], axis=1)
        feat = (feat + both).astype(BF16)
        dec_ref[jnp.minimum(2 * m, slab_height - 1)] = feat[all_out:, 128:]
        dec_ref[jnp.abs(2 * m - 1)] = feat[all_out:, :128]
        value = feat[:all_out, :].astype(F32)
        halved = 0.5 * value
        buf[...] = (halved + halved * jnp.tanh(halved)).astype(BF16)

    def multiply(m, buf, slot):
        tap = jnp.dot(w1_ref[...], buf[...], preferred_element_type=F32)
        slot[0] = tap[:, :128]
        slot[1] = tap[:, 128:]

    def finish(m, before, slot):
        lines = (before.at[0], before.at[1], slot.at[0], slot.at[1])
        for n in range(2):
            y = 2 * m - 2 + n
            global_row = lax.rem(first_row + y, WPIX)
            sums = lines[n + 1][3 * outs : 6 * outs, :]
            sums = sums + jnp.where(global_row != 0, lines[n][0 : 3 * outs, :], 0.0)
            sums = sums + jnp.where(global_row != WPIX - 1, lines[n + 2][6 * outs :, :], 0.0)
            total = sums[outs : 2 * outs, :] + b1_ref[...]
            total = total + jnp.where(lane == 0, 0.0, pltpu.roll(sums[0:outs, :], 1, 1))
            total = total + jnp.where(lane == 127, 0.0, pltpu.roll(sums[2 * outs :, :], 127, 1))
            res_ref[y] = total.astype(BF16)

    acts = (act, act2)
    features(0, act)
    tap2[...] = jnp.zeros_like(tap2)
    tap3[...] = jnp.zeros_like(tap3)
    taps = (tap0, tap1, tap2, tap3)

    def several(step, carry):
        for n in range(12):
            m = 12 * step + 1 + n
            finish(jnp.maximum(m - 2, 1), taps[(n + 2) % 4], taps[(n + 3) % 4])
            features(m, acts[(n + 1) % 2])
            multiply(m - 1, acts[n % 2], taps[n % 4])
        return carry

    lax.fori_loop(0, rows // 12, several, 0)
    finish(rows - 1, taps[(rows - 2) % 4], taps[(rows - 1) % 4])
    multiply(rows, acts[rows % 2], taps[rows % 4])
    finish(rows, taps[(rows - 1) % 4], taps[rows % 4])


SPACES = {"s": pltpu.SMEM, "v": pltpu.VMEM, "h": pltpu.HBM}


def call(body, inputs, kinds, out_shape, scratch, flops, bytes_accessed, limit):
    return pl.pallas_call(
        body,
        out_shape=out_shape,
        in_specs=[pl.BlockSpec(memory_space=SPACES[k]) for k in kinds],
        out_specs=jax.tree.map(lambda _: pl.BlockSpec(memory_space=pltpu.VMEM), out_shape),
        scratch_shapes=scratch,
        compiler_params=pltpu.CompilerParams(vmem_limit_bytes=limit << 20),
        cost_estimate=pl.CostEstimate(flops=flops, bytes_accessed=bytes_accessed, transcendentals=0),
    )(*inputs)


def decode_call(rows, here, latents, weight, bias, w1, b1):
    width = latents.shape[1]
    outs = w1.shape[0] // 9
    channels = w1.shape[1]
    shape = jax.ShapeDtypeStruct((2 * rows, outs, WPIX), BF16)
    return call(
        functools.partial(decode_kernel, rows),
        (here, latents, weight, bias, w1, b1),
        "svvvvv",
        (shape, shape),
        [
            pltpu.VMEM((width, 512), F32),
            pltpu.VMEM((2 * (rows + 2) * 48, 128), BF16),
            pltpu.VMEM((channels, 256), BF16),
            pltpu.VMEM((channels, 256), BF16),
        ]
        + [pltpu.VMEM((2, 9 * outs, 128), F32)] * 4,
        6 * 10**9,
        3 * 10**6,
        24,
    )


def gather_call(here, recv, peers, outs):
    sds = jax.ShapeDtypeStruct
    many = (peers + 1) * outs
    return call(
        functools.partial(gather_kernel, peers),
        (here, recv),
        "sv",
        (sds((many, 144), BF16), sds((many, 128), F32)),
        [],
        10**6,
        10**6,
        8,
    )


def project_call(rows, peers, hidden, small):
    large = (hidden,) + small
    return call(
        functools.partial(project_kernel, rows, peers),
        large,
        "hhhhh",
        (jax.ShapeDtypeStruct((peers * BLOCK, 128), BF16), jax.ShapeDtypeStruct((WBLOCK, 128), BF16)),
        [pltpu.VMEM(x.shape, x.dtype) for x in large]
        + [pltpu.VMEM((hidden.shape[1], 128), F32), pltpu.SemaphoreType.DMA((5,))],
        10**9,
        2 * 10**6,
        60,
    )


def clean_call(peers, slabs, feats, recv, side, route):
    return call(
        functools.partial(clean_kernel, peers, feats),
        (recv, side, route),
        "vvv",
        jax.ShapeDtypeStruct((slabs * 8, 128), BF16),
        [],
        10**7,
        10**6,
        8,
    )


def pick_call(peers, choose, landed):
    return call(
        functools.partial(pick_kernel, peers),
        (choose, landed),
        "vv",
        jax.ShapeDtypeStruct((peers * 8, choose.shape[0] // 32 * 128), BF16),
        [],
        10**7,
        10**6,
        8,
    )


def shards(
    hidden,
    modulation,
    final_weight,
    noisy,
    step_index,
    slab_table,
    conv_in_weight,
    conv_in_bias,
    conv1_weight,
    conv1_bias,
):
    peers = lax.axis_size("tensor")
    slabs = lax.axis_size("wide")
    t = lax.axis_index("tensor")
    w = lax.axis_index("wide")
    here = jnp.concatenate([jnp.stack([t, w]).astype(jnp.int32), step_index, slab_table])
    rows = slab_table.shape[0]
    feats = hidden.shape[1]
    outs = conv_in_weight.shape[1]
    sds = jax.ShapeDtypeStruct
    small = (modulation, final_weight.T, conv_in_weight.T, conv_in_bias.reshape(1, -1))
    send, shard = project_call(rows, peers, hidden.T, small)
    blocks = ((rows + 2) // 2 + 1) // 2
    side, route, choose = call(
        functools.partial(side_kernel, rows, peers, slabs),
        (here, noisy.T),
        "sv",
        (sds((2 * SR + 8, 128), F32), sds((2 * slabs * 8, 128), BF16), sds((4 * blocks * 8, slabs * 8), BF16)),
        [pltpu.VMEM(noisy.shape, F32)],
        10**6,
        10**6,
        8,
    )
    recv = lax.all_to_all(send, "tensor", split_axis=0, concat_axis=0, tiled=True)
    routed = clean_call(peers, slabs, feats, recv, side, route)

    landed = lax.all_to_all(routed, "wide", split_axis=0, concat_axis=0, tiled=True)
    for bit in STEPS_AWAY:
        pairs = [(i, i ^ bit) for i in range(peers)]
        shard = jnp.concatenate([shard, lax.ppermute(shard, "tensor", pairs)], axis=0)
    copies = pick_call(peers, choose, landed)
    latents = lax.all_to_all(copies, "tensor", split_axis=0, concat_axis=0, tiled=True)
    own = lax.dynamic_slice_in_dim(conv1_weight, t * outs, outs, 2)
    w1 = own.transpose(0, 2, 1).reshape(9 * outs, -1)
    b1 = jnp.broadcast_to(lax.dynamic_slice_in_dim(conv1_bias, t * outs, outs, 0)[:, None], (outs, 128))
    weight, bias = gather_call(here, shard, peers, outs)
    return decode_call(rows, here, latents, weight, bias, w1, b1)


def solution(mesh):
    return jax.shard_map(
        shards,
        mesh=mesh,
        in_specs=(
            P("wide", "tensor"),
            P(None, "tensor"),
            P("tensor", None),
            P("wide", None),
            P(),
            P("wide"),
            P(None, "tensor"),
            P("tensor"),
            P(),
            P(),
        ),
        out_specs=(P("wide", "tensor", None), P("wide", "tensor", None)),
        check_vma=False,
    )
```
